128 devices in a mesh: gx: 16 (over z, y_lo, core), gy: 8 (over y_hi, x).
Axes of the slice: x: 4, y: 4 (y_hi: 2, y_lo: 2; y = y_hi * 2 + y_lo), z: 4, core: 2. Of those that a mesh axis runs over, the one named last changes fastest.
Arguments:
- observed: float32 [16, 32768], P(None, ('gx', 'gy')), may hold values from -24 to 24
- synthetic: float32 [32, 32768], P(None, ('gx', 'gy')), may hold values from -24 to 24
- match_filter: float32 [16, 17], replicated, may hold values from -1.8 to 1.8
- trace_shot: int32 [32768], P(('gx', 'gy')), may hold values from 0 to 15
- trace_owner: int32 [32768, 1], P(('gx', 'gy')), may hold values from 0 to 127; in each aligned block of 256 rows (0 to 255, 256 to 511, ...) at most 4 rows name the same one
- trace_cell: int32 [32768], P(('gx', 'gy')), may hold values from 0 to 262143
- courant: float32 [512, 256, 256], P('gx', 'gy'), may hold values from 0.05 to 0.18
- adjoint_now: float32 [512, 256, 256], P('gx', 'gy'), may hold values from -6 to 6
- adjoint_prev: float32 [512, 256, 256], P('gx', 'gy'), may hold values from -6 to 6
- forward_field: bfloat16 [16, 512, 256, 256], P(None, 'gx', 'gy'), may hold values from -6 to 6
- image_start: float32 [512, 256, 256], P('gx', 'gy'), may hold values from -6 to 6
Outputs:
- adjoint_field: float32 [512, 256, 256], P('gx', 'gy')
- adjoint_before: float32 [512, 256, 256], P('gx', 'gy')
- gradient_image: float32 [512, 256, 256], P('gx', 'gy')
The draws below stay inside these ranges and needn't reach their ends.
Inputs may be any that keep to these rules, and one draw needn't show every extreme that they name: `trace_owner`: among the rows of one device, no owner appears more than 4 times. `trace_cell`: local cell number (a * 32 + b) * 256 + z of the receiver inside its owner's block.
All inputs are finite; a program needn't handle non-finite values.
Results may differ from the reference program's by a relative error of at most 0.0003.
Values sent between devices are 32-bit elements; how exact they have to be, the bound alone decides.
A program may use at most 128 MiB of HBM per device.

```python
import math
import jax
import jax.numpy as jnp
import numpy as np

CX = 32
CY = 32
NZ = 256
TR_DEV = 256
STEPS = 16
SHOTS = 16
TAPS = 17
NX = 512
NY = 256
TRACES = 32768
CAP = 4
N_GY = 8
DEVICES = 128


def touch_ends(array, own_key, smallest, high):
    shape = array.shape
    place = [jax.random.randint(jax.random.fold_in(own_key, axis), (), 0, shape[axis]) for axis in range(len(shape))]
    array = array.at[tuple(place)].set(smallest)
    longest = shape.index(max(shape))
    place[longest] = (place[longest] + 1) % shape[longest]
    return array.at[tuple(place)].set(high)


def block_levels(stream_key, shape, cuts, low, largest):
    def one(axis_at, shards_of):
        steps = jax.random.uniform(jax.random.fold_in(jax.random.fold_in(stream_key, 6), axis_at), (shards_of,), jnp.float32, low / len(cuts), largest / len(cuts))
        return jnp.repeat(jnp.exp(steps), shape[axis_at] // shards_of).reshape((-1,) + (1,) * (len(shape) - axis_at - 1))

    level = one(*cuts[0])
    for cut in cuts[1:]:
        level = level * one(*cut)
    return level


def routed_block(key, own, number, rows, number_of, top, limit, lean):
    order = jax.random.permutation(key, number_of)
    packed, usual = shares(number_of, rows * top, limit, lean, True), shares(number_of, rows * top, limit, lean, False)
    places = jnp.arange(number_of)

    def named(sizes, offset_by):
        used = int((sizes > 0).sum())
        fixed = max(1, used // 4)
        moved = fixed + (places - fixed + offset_by * (used - fixed)) % max(1, number_of - fixed)
        return jnp.zeros((number_of,), jnp.int32).at[order[jnp.where(places < fixed, places, moved)]].set(jnp.asarray(sizes, jnp.int32))

    sizes = jnp.where(number % 4 == 0, named(packed, number // 4), named(usual, number - number // 4 - 1))
    mixed = jax.random.permutation(jax.random.fold_in(own, 3), number_of)
    giver, receiver = mixed[0:number_of // 2 * 2:2], mixed[1:number_of // 2 * 2:2]
    margin = jnp.minimum(sizes[giver] - 1, limit - sizes[receiver]) // 2
    margin = jnp.where((giver == order[0]) | (receiver == order[0]) | (sizes[receiver] == 0), 0, jnp.maximum(margin, 0))
    moved = jax.random.randint(jax.random.fold_in(own, 4), (number_of // 2,), 0, 1 << 20) % (margin + 1)
    sizes = sizes.at[giver].add(-moved).at[receiver].add(moved)
    labels = jnp.searchsorted(jnp.cumsum(sizes), jnp.arange(rows * top), side="right").astype(jnp.int32)
    listing = labels.reshape(top, rows).T
    listing = listing[jax.random.permutation(jax.random.fold_in(own, 1), rows)]
    offset_by = jax.random.randint(jax.random.fold_in(own, 2), (rows, 1), 0, top)
    return jnp.take_along_axis(listing, (jnp.arange(top)[None, :] + offset_by) % top, axis=1)


def shares(amount, total, reach, lean, full):
    loads = [(1 << 20) // math.isqrt(grade ** lean) + 1 for grade in range(1, amount + 1)]
    largest = reach if full else min(reach, max(-(-total // amount), total * loads[0] // sum(loads)))
    least = 1 if total - largest >= amount - 1 else 0
    counts, rest = [largest] + [least] * (amount - 1), total - largest - least * (amount - 1)
    while rest > 0:
        free = [i for i in range(1, amount) if counts[i] < largest] or [i for i in range(1, amount) if counts[i] < reach]
        whole, remaining = sum([loads[i] for i in free]), rest
        for i in free:
            more = min(reach - counts[i], max(1, remaining * loads[i] // whole), rest)
            counts[i] = counts[i] + more
            rest = rest - more
    return np.array(counts)


def gaussian(rng, extent, scale, most, split=(), kind=jnp.bfloat16):
    gain = block_levels(rng, extent, split, -0.22, 0.18) if split else 1.0
    result = jax.random.normal(rng, extent, jnp.float32) * scale * gain
    return jnp.minimum(jnp.maximum(result, -most), most).astype(kind)


def setup_inputs(seed: int = 0) -> dict:
    keys = jax.random.split(jax.random.key(seed), 12)
    observed = gaussian(keys[0], (STEPS, TRACES), 4.0, 24.0, ((1, 128),), jnp.float32)
    synthetic = gaussian(keys[1], (2 * STEPS, TRACES), 4.0, 24.0, ((1, 128),), jnp.float32)
    match_filter = gaussian(keys[2], (SHOTS, TAPS), 0.3, 1.8, (), jnp.float32)
    trace_shot = touch_ends(jax.random.randint(keys[3], (TRACES,), 0, SHOTS), jax.random.fold_in(keys[3], 1), 0, SHOTS - 1).astype(jnp.int32)
    trace_owner_keys = jax.random.split(jax.random.fold_in(keys[4], 1), TRACES // TR_DEV)
    trace_owner_turns = jax.random.permutation(jax.random.fold_in(keys[4], 3), TRACES // TR_DEV)
    trace_owner = jax.vmap(lambda own, number: routed_block(jax.random.fold_in(keys[4], 2), own, number, TR_DEV, DEVICES, 1, CAP, 2))(trace_owner_keys, trace_owner_turns).reshape((TRACES, 1))
    trace_cell = touch_ends(jax.random.randint(keys[5], (TRACES,), 0, CX * CY * NZ), jax.random.fold_in(keys[5], 1), 0, (CX * CY * NZ) - 1).astype(jnp.int32)
    courant = jnp.clip(0.05 + 0.13000001 * jax.random.uniform(keys[6], (NX, NY, NZ), jnp.float32) ** block_levels(keys[6], (NX, NY, NZ), ((0, 16), (1, 8)), -0.2, 0.2), 0.05, 0.18)
    adjoint_now = gaussian(keys[7], (NX, NY, NZ), 1.0, 6.0, ((0, 16), (1, 8)), jnp.float32)
    adjoint_prev = gaussian(keys[8], (NX, NY, NZ), 1.0, 6.0, ((0, 16), (1, 8)), jnp.float32)
    forward_field = gaussian(keys[9], (STEPS, NX, NY, NZ), 1.0, 6.0, ((1, 16), (2, 8)))
    image_start = gaussian(keys[10], (NX, NY, NZ), 1.0, 6.0, ((0, 16), (1, 8)), jnp.float32)
    return dict(observed=observed, synthetic=synthetic, match_filter=match_filter, trace_shot=trace_shot, trace_owner=trace_owner, trace_cell=trace_cell, courant=courant, adjoint_now=adjoint_now, adjoint_prev=adjoint_prev, forward_field=forward_field, image_start=image_start)


stencil_weights = (-205.0 / 72.0, 8.0 / 5.0, -1.0 / 5.0, 8.0 / 315.0, -1.0 / 560.0)


def laplace(padded):
    width_x = padded.shape[0] - 8
    width_y = padded.shape[1] - 8
    center = padded[4:4 + width_x, 4:4 + width_y]
    column = center.shape[2]
    z_padded = jnp.pad(center, ((0, 0), (0, 0), (4, 4)))
    summed = 3.0 * stencil_weights[0] * center
    for offset in range(1, 5):
        along_x = padded[4 + offset:4 + offset + width_x, 4:4 + width_y] + padded[4 - offset:4 - offset + width_x, 4:4 + width_y]
        along_y = padded[4:4 + width_x, 4 + offset:4 + offset + width_y] + padded[4:4 + width_x, 4 - offset:4 - offset + width_y]
        along_z = z_padded[:, :, 4 + offset:4 + offset + column] + z_padded[:, :, 4 - offset:4 - offset + column]
        summed = summed + stencil_weights[offset] * (along_x + along_y + along_z)
    return summed


def reference(observed, synthetic, match_filter, trace_shot, trace_owner, trace_cell, courant, adjoint_now, adjoint_prev, forward_field, image_start):
    filters = jnp.take(match_filter, trace_shot, axis=0).T
    residual = -observed
    for lag_index in range(TAPS):
        residual = residual + filters[lag_index][None, :] * synthetic[STEPS - lag_index:2 * STEPS - lag_index]
    owners = trace_owner[:, 0]
    local_x = trace_cell // (CY * NZ)
    local_y = (trace_cell // NZ) % CY
    local_z = trace_cell % NZ
    global_x = (owners // N_GY) * CX + local_x
    global_y = (owners % N_GY) * CY + local_y
    flat_cell = ((global_x * NY + global_y) * NZ + local_z).astype(jnp.int32)
    current = adjoint_now
    before = adjoint_prev
    imaging = image_start
    for position in range(STEPS):
        source = jnp.zeros((NX * NY * NZ,), jnp.float32).at[flat_cell].add(residual[STEPS - 1 - position]).reshape(NX, NY, NZ)
        padded = jnp.pad(current, ((4, 4), (4, 4), (0, 0)))
        following = 2.0 * current - before + courant * (laplace(padded) + source)
        imaging = imaging + forward_field[position].astype(jnp.float32) * following
        before = current
        current = following
    return (current, before, imaging)
```

```python
import jax
import jax.numpy as jnp
from jax import lax
from jax.sharding import PartitionSpec as P

STEPS = 16
SHOTS = 16
TAPS = 17
HALO = 4


stencil_weights = (-205.0 / 72.0, 8.0 / 5.0, -1.0 / 5.0, 8.0 / 315.0, -1.0 / 560.0)


def faces(value, axis, dim):
    peers, length = lax.axis_size(axis), value.shape[dim]
    up = [(i, i + 1) for i in range(peers - 1)]
    down = [(j, i) for i, j in up]
    last = lax.slice_in_dim(value, length - HALO, length, axis=dim)
    first = lax.slice_in_dim(value, 0, HALO, axis=dim)
    return lax.ppermute(last, axis, up), lax.ppermute(first, axis, down)


def laplace(center, x_lo, x_hi, y_lo, y_hi):
    width_x, width_y, column = center.shape
    along_x_src = jnp.concatenate([x_lo, center, x_hi], axis=0)
    along_y_src = jnp.concatenate([y_lo, center, y_hi], axis=1)
    z_padded = jnp.pad(center, ((0, 0), (0, 0), (4, 4)))
    summed = 3.0 * stencil_weights[0] * center
    for offset in range(1, 5):
        along_x = (
            along_x_src[4 + offset : 4 + offset + width_x]
            + along_x_src[4 - offset : 4 - offset + width_x]
        )
        along_y = (
            along_y_src[:, 4 + offset : 4 + offset + width_y]
            + along_y_src[:, 4 - offset : 4 - offset + width_y]
        )
        along_z = (
            z_padded[:, :, 4 + offset : 4 + offset + column]
            + z_padded[:, :, 4 - offset : 4 - offset + column]
        )
        summed = summed + stencil_weights[offset] * (along_x + along_y + along_z)
    return summed


def per_device(
    observed,
    synthetic,
    match_filter,
    trace_shot,
    trace_owner,
    trace_cell,
    courant,
    adjoint_now,
    adjoint_prev,
    forward_field,
    image_start,
):
    trace_rows = observed.shape[1]
    grid_x = lax.axis_size("gx")
    grid_y = lax.axis_size("gy")
    devices = grid_x * grid_y
    capacity = max(2, 2 * trace_rows // devices)
    slot_count = devices * capacity
    shot_match = (trace_shot[:, None] == jnp.arange(SHOTS, dtype=jnp.int32)[None, :]).astype(
        jnp.float32
    )
    filters = jnp.dot(match_filter.T, shot_match.T, precision=lax.Precision.HIGHEST)
    residual = -observed
    for lag_index in range(TAPS):
        residual = (
            residual
            + filters[lag_index][None, :] * synthetic[STEPS - lag_index : 2 * STEPS - lag_index]
        )
    owners = trace_owner[:, 0]
    same_owner = owners[:, None] == owners[None, :]
    row_ids = jnp.arange(trace_rows, dtype=jnp.int32)
    earlier = row_ids[None, :] < row_ids[:, None]
    ranks = jnp.sum((same_owner & earlier).astype(jnp.int32), axis=1)
    slot_index = owners * capacity + ranks
    slot_table = (slot_index[:, None] == jnp.arange(slot_count, dtype=jnp.int32)[None, :]).astype(
        jnp.float32
    )
    payload = jnp.concatenate([residual, trace_cell.astype(jnp.float32)[None, :]], axis=0)
    parcel = jnp.dot(payload, slot_table, precision=lax.Precision.HIGHEST)
    received = lax.all_to_all(parcel, ("gx", "gy"), split_axis=1, concat_axis=1, tiled=True)
    got_values = received[:STEPS][::-1]
    got_cells = received[STEPS].astype(jnp.int32)
    plane = courant.shape[0] * courant.shape[1]
    column = courant.shape[2]
    got_plane = got_cells // column
    got_depth = got_cells % column
    at_plane = (got_plane[None, :] == jnp.arange(plane, dtype=jnp.int32)[:, None]).astype(jnp.bfloat16)
    at_plane = jnp.concatenate([at_plane] * 3, axis=1)
    at_depth = got_depth[:, None] == jnp.arange(column, dtype=jnp.int32)[None, :]
    at_depth = jnp.concatenate([at_depth] * 3, axis=0)
    high = got_values.astype(jnp.bfloat16)
    rest = got_values - high.astype(jnp.float32)
    middle = rest.astype(jnp.bfloat16)
    low = (rest - middle.astype(jnp.float32)).astype(jnp.bfloat16)
    pieces = jnp.concatenate([high, middle, low], axis=1)

    def advance(position, carry):
        current, before, imaging = carry
        x_lo, x_hi = faces(current, "gx", 0)
        y_lo, y_hi = faces(current, "gy", 1)
        piece = lax.dynamic_index_in_dim(pieces, position, 0, keepdims=False)
        spread = jnp.where(at_depth, piece[:, None], jnp.zeros((), jnp.bfloat16))
        source = jnp.dot(at_plane, spread, preferred_element_type=jnp.float32).reshape(
            current.shape
        )
        following = 2.0 * current - before + courant * (
            laplace(current, x_lo, x_hi, y_lo, y_hi) + source
        )
        snapshot = lax.dynamic_index_in_dim(forward_field, position, 0, keepdims=False)
        imaging = imaging + snapshot.astype(jnp.float32) * following
        return (following, current, imaging)

    current, before, imaging = lax.fori_loop(
        0, STEPS, advance, (adjoint_now, adjoint_prev, image_start)
    )
    return (current, before, imaging)


def solution(mesh):
    return jax.shard_map(
        per_device,
        mesh=mesh,
        in_specs=(
            P(None, ("gx", "gy")),
            P(None, ("gx", "gy")),
            P(),
            P(("gx", "gy")),
            P(("gx", "gy"), None),
            P(("gx", "gy")),
            P("gx", "gy", None),
            P("gx", "gy", None),
            P("gx", "gy", None),
            P(None, "gx", "gy", None),
            P("gx", "gy", None),
        ),
        out_specs=(P("gx", "gy", None), P("gx", "gy", None), P("gx", "gy", None)),
        check_vma=False,
    )
```

```python
import jax
import jax.numpy as jnp
from jax import lax
from jax.sharding import PartitionSpec as P

STEPS = 16
SHOTS = 16
TAPS = 17
HALO = 4


stencil_weights = (-205.0 / 72.0, 8.0 / 5.0, -1.0 / 5.0, 8.0 / 315.0, -1.0 / 560.0)


def faces(value, axis, dim):
    peers, length = lax.axis_size(axis), value.shape[dim]
    up = [(i, i + 1) for i in range(peers - 1)]
    down = [(j, i) for i, j in up]
    last = lax.slice_in_dim(value, length - HALO, length, axis=dim)
    first = lax.slice_in_dim(value, 0, HALO, axis=dim)
    return lax.ppermute(last, axis, up), lax.ppermute(first, axis, down)


def split_high(value):
    scaled = value * 65537.0
    return scaled - (scaled - value)


def laplace(center, x_lo, x_hi, y_lo, y_hi):
    width_x, width_y, column = center.shape
    along_x_src = jnp.concatenate([x_lo, center, x_hi], axis=0)
    along_y_src = jnp.concatenate([y_lo, center, y_hi], axis=1)
    z_padded = jnp.pad(center, ((0, 0), (0, 0), (4, 4)))
    summed = 3.0 * stencil_weights[0] * center
    for offset in range(1, 5):
        along_x = (
            along_x_src[4 + offset : 4 + offset + width_x]
            + along_x_src[4 - offset : 4 - offset + width_x]
        )
        along_y = (
            along_y_src[:, 4 + offset : 4 + offset + width_y]
            + along_y_src[:, 4 - offset : 4 - offset + width_y]
        )
        along_z = (
            z_padded[:, :, 4 + offset : 4 + offset + column]
            + z_padded[:, :, 4 - offset : 4 - offset + column]
        )
        summed = summed + stencil_weights[offset] * (along_x + along_y + along_z)
    return summed


def per_device(
    observed,
    synthetic,
    match_filter,
    trace_shot,
    trace_owner,
    trace_cell,
    courant,
    adjoint_now,
    adjoint_prev,
    forward_field,
    image_start,
):
    trace_rows = observed.shape[1]
    grid_x = lax.axis_size("gx")
    grid_y = lax.axis_size("gy")
    devices = grid_x * grid_y
    capacity = max(2, 2 * trace_rows // devices)
    slot_count = devices * capacity
    shot_match = (trace_shot[:, None] == jnp.arange(SHOTS, dtype=jnp.int32)[None, :]).astype(
        jnp.float32
    )
    filters = jnp.dot(match_filter.T, shot_match.T, precision=lax.Precision.HIGHEST)
    residual = -observed
    for lag_index in range(TAPS):
        residual = (
            residual
            + filters[lag_index][None, :] * synthetic[STEPS - lag_index : 2 * STEPS - lag_index]
        )
    owners = trace_owner[:, 0]
    same_owner = owners[:, None] == owners[None, :]
    row_ids = jnp.arange(trace_rows, dtype=jnp.int32)
    earlier = row_ids[None, :] < row_ids[:, None]
    ranks = jnp.sum((same_owner & earlier).astype(jnp.int32), axis=1)
    slot_index = owners * capacity + ranks
    slot_table = (slot_index[:, None] == jnp.arange(slot_count, dtype=jnp.int32)[None, :]).astype(
        jnp.float32
    )
    payload = jnp.concatenate([residual, trace_cell.astype(jnp.float32)[None, :]], axis=0)
    parcel = jnp.dot(payload, slot_table, precision=lax.Precision.HIGHEST)
    received = lax.all_to_all(parcel, ("gx", "gy"), split_axis=1, concat_axis=1, tiled=True)
    got_values = received[:STEPS][::-1]
    got_cells = received[STEPS].astype(jnp.int32)
    plane = courant.shape[0] * courant.shape[1]
    column = courant.shape[2]
    got_plane = got_cells // column
    got_depth = got_cells % column
    at_plane = (got_plane[:, None] == jnp.arange(plane, dtype=jnp.int32)[None, :]).astype(jnp.bfloat16)
    at_plane = jnp.concatenate([at_plane] * 3, axis=0)
    at_depth = got_depth[:, None] == jnp.arange(column, dtype=jnp.int32)[None, :]
    at_depth = jnp.concatenate([at_depth] * 3, axis=0)
    top = split_high(got_values)
    rest = got_values - top
    second = split_high(rest)
    pieces = jnp.concatenate([top, second, rest - second], axis=1).astype(jnp.bfloat16)

    def advance(position, carry):
        current, before, imaging = carry
        x_lo, x_hi = faces(current, "gx", 0)
        y_lo, y_hi = faces(current, "gy", 1)
        piece = lax.dynamic_index_in_dim(pieces, position, 0, keepdims=False)
        spread = jnp.where(at_depth, piece[:, None], jnp.zeros((), jnp.bfloat16))
        source = lax.dot_general(
            spread, at_plane, (((0,), (0,)), ((), ())), preferred_element_type=jnp.float32
        ).T.reshape(current.shape)
        following = 2.0 * current - before + courant * (
            laplace(current, x_lo, x_hi, y_lo, y_hi) + source
        )
        snapshot = lax.dynamic_index_in_dim(forward_field, position, 0, keepdims=False)
        imaging = imaging + snapshot.astype(jnp.float32) * following
        return (following, current, imaging)

    current, before, imaging = lax.fori_loop(
        0, STEPS, advance, (adjoint_now, adjoint_prev, image_start)
    )
    return (current, before, imaging)


def solution(mesh):
    return jax.shard_map(
        per_device,
        mesh=mesh,
        in_specs=(
            P(None, ("gx", "gy")),
            P(None, ("gx", "gy")),
            P(),
            P(("gx", "gy")),
            P(("gx", "gy"), None),
            P(("gx", "gy")),
            P("gx", "gy", None),
            P("gx", "gy", None),
            P("gx", "gy", None),
            P(None, "gx", "gy", None),
            P("gx", "gy", None),
        ),
        out_specs=(P("gx", "gy", None), P("gx", "gy", None), P("gx", "gy", None)),
        check_vma=False,
    )
```

```python
import functools

import jax
import jax.numpy as jnp
from jax import lax
from jax.experimental import pallas as pl
from jax.experimental.pallas import tpu as pltpu
from jax.sharding import PartitionSpec as P

MESH = pl.DeviceIdType.MESH

STEPS = 16
SHOTS = 16
TAPS = 17
HALO = 4


stencil_weights = (-205.0 / 72.0, 8.0 / 5.0, -1.0 / 5.0, 8.0 / 315.0, -1.0 / 560.0)


def faces(value, axis, dim):
    peers, length = lax.axis_size(axis), value.shape[dim]
    up = [(i, i + 1) for i in range(peers - 1)]
    down = [(j, i) for i, j in up]
    last = lax.slice_in_dim(value, length - HALO, length, axis=dim)
    first = lax.slice_in_dim(value, 0, HALO, axis=dim)
    return lax.ppermute(last, axis, up), lax.ppermute(first, axis, down)


def exchange_kernel(grid_x, grid_y, cur_ref, x_lo_ref, x_hi_ref, y_lo_ref, y_hi_ref, held_x, held_y, send_sem, recv_sem):
    me_x = lax.axis_index("gx")
    me_y = lax.axis_index("gy")
    width_x, width_y, _ = cur_ref.shape
    has = (me_x > 0, me_x < grid_x - 1, me_y > 0, me_y < grid_y - 1)
    peers = ((me_x - 1, me_y), (me_x + 1, me_y), (me_x, me_y - 1), (me_x, me_y + 1))
    count = sum(flag.astype(jnp.int32) for flag in has)

    barrier = pltpu.get_barrier_semaphore()
    for flag, peer in zip(has, peers):
        @pl.when(flag)
        def _():
            pl.semaphore_signal(barrier, inc=1, device_id=peer, device_id_type=MESH)
    pl.semaphore_wait(barrier, count)

    sources = (
        cur_ref.at[pl.ds(0, HALO)],
        cur_ref.at[pl.ds(width_x - HALO, HALO)],
        cur_ref.at[:, pl.ds(0, HALO)],
        cur_ref.at[:, pl.ds(width_y - HALO, HALO)],
    )
    targets = (held_x.at[1], held_x.at[0], held_y.at[1], held_y.at[0])
    face_of = (1, 0, 3, 2)

    def copy_to(side):
        face = face_of[side]
        return pltpu.make_async_remote_copy(
            src_ref=sources[side],
            dst_ref=targets[side],
            send_sem=send_sem.at[side],
            recv_sem=recv_sem.at[face],
            device_id=peers[side],
            device_id_type=MESH,
        )

    for side in range(4):
        @pl.when(has[side])
        def _():
            copy_to(side).start()

    for side in range(4):
        @pl.when(has[side])
        def _():
            copy_to(side).wait_send()

    arriving = (copy_to(1), copy_to(0), copy_to(3), copy_to(2))
    outs = (x_lo_ref, x_hi_ref, y_lo_ref, y_hi_ref)
    landed = (held_x.at[0], held_x.at[1], held_y.at[0], held_y.at[1])
    for face in range(4):
        @pl.when(has[face])
        def _():
            arriving[face].wait_recv()
            outs[face][...] = landed[face][...]

        @pl.when(jnp.logical_not(has[face]))
        def _():
            outs[face][...] = jnp.zeros(outs[face].shape, outs[face].dtype)


def exchange(current):
    grid_x, grid_y = lax.axis_size("gx"), lax.axis_size("gy")
    width_x, width_y, column = current.shape
    x_face = jax.ShapeDtypeStruct((HALO, width_y, column), current.dtype)
    y_face = jax.ShapeDtypeStruct((width_x, HALO, column), current.dtype)
    vmem = pl.BlockSpec(memory_space=pltpu.VMEM)
    return pl.pallas_call(
        functools.partial(exchange_kernel, grid_x, grid_y),
        out_shape=(x_face, x_face, y_face, y_face),
        in_specs=[pl.BlockSpec(memory_space=pl.ANY)],
        out_specs=(vmem, vmem, vmem, vmem),
        scratch_shapes=[
            pltpu.VMEM((2, HALO, width_y, column), current.dtype),
            pltpu.VMEM((2, width_x, HALO, column), current.dtype),
            pltpu.SemaphoreType.DMA((4,)),
            pltpu.SemaphoreType.DMA((4,)),
        ],
        compiler_params=pltpu.CompilerParams(collective_id=0, has_side_effects=True),
    )(current)


def split_high(value):
    scaled = value * 65537.0
    return scaled - (scaled - value)


def laplace(center, x_lo, x_hi, y_lo, y_hi):
    width_x, width_y, column = center.shape
    along_x_src = jnp.concatenate([x_lo, center, x_hi], axis=0)
    along_y_src = jnp.concatenate([y_lo, center, y_hi], axis=1)
    z_padded = jnp.pad(center, ((0, 0), (0, 0), (4, 4)))
    summed = 3.0 * stencil_weights[0] * center
    for offset in range(1, 5):
        along_x = (
            along_x_src[4 + offset : 4 + offset + width_x]
            + along_x_src[4 - offset : 4 - offset + width_x]
        )
        along_y = (
            along_y_src[:, 4 + offset : 4 + offset + width_y]
            + along_y_src[:, 4 - offset : 4 - offset + width_y]
        )
        along_z = (
            z_padded[:, :, 4 + offset : 4 + offset + column]
            + z_padded[:, :, 4 - offset : 4 - offset + column]
        )
        summed = summed + stencil_weights[offset] * (along_x + along_y + along_z)
    return summed


def per_device(
    observed,
    synthetic,
    match_filter,
    trace_shot,
    trace_owner,
    trace_cell,
    courant,
    adjoint_now,
    adjoint_prev,
    forward_field,
    image_start,
):
    trace_rows = observed.shape[1]
    grid_x = lax.axis_size("gx")
    grid_y = lax.axis_size("gy")
    devices = grid_x * grid_y
    capacity = max(2, 2 * trace_rows // devices)
    slot_count = devices * capacity
    shot_match = (trace_shot[:, None] == jnp.arange(SHOTS, dtype=jnp.int32)[None, :]).astype(
        jnp.float32
    )
    filters = jnp.dot(match_filter.T, shot_match.T, precision=lax.Precision.HIGHEST)
    residual = -observed
    for lag_index in range(TAPS):
        residual = (
            residual
            + filters[lag_index][None, :] * synthetic[STEPS - lag_index : 2 * STEPS - lag_index]
        )
    owners = trace_owner[:, 0]
    same_owner = owners[:, None] == owners[None, :]
    row_ids = jnp.arange(trace_rows, dtype=jnp.int32)
    earlier = row_ids[None, :] < row_ids[:, None]
    ranks = jnp.sum((same_owner & earlier).astype(jnp.int32), axis=1)
    slot_index = owners * capacity + ranks
    slot_table = (slot_index[:, None] == jnp.arange(slot_count, dtype=jnp.int32)[None, :]).astype(
        jnp.float32
    )
    payload = jnp.concatenate([residual, trace_cell.astype(jnp.float32)[None, :]], axis=0)
    parcel = jnp.dot(payload, slot_table, precision=lax.Precision.HIGHEST)
    received = lax.all_to_all(parcel, ("gx", "gy"), split_axis=1, concat_axis=1, tiled=True)
    got_values = received[:STEPS][::-1]
    got_cells = received[STEPS].astype(jnp.int32)
    plane = courant.shape[0] * courant.shape[1]
    column = courant.shape[2]
    got_plane = got_cells // column
    got_depth = got_cells % column
    at_plane = (got_plane[:, None] == jnp.arange(plane, dtype=jnp.int32)[None, :]).astype(jnp.bfloat16)
    at_plane = jnp.concatenate([at_plane] * 3, axis=0)
    at_depth = got_depth[:, None] == jnp.arange(column, dtype=jnp.int32)[None, :]
    at_depth = jnp.concatenate([at_depth] * 3, axis=0)
    top = split_high(got_values)
    rest = got_values - top
    second = split_high(rest)
    pieces = jnp.concatenate([top, second, rest - second], axis=1).astype(jnp.bfloat16)

    def advance(position, carry):
        current, before, imaging = carry
        x_lo, x_hi, y_lo, y_hi = exchange(current)
        piece = lax.dynamic_index_in_dim(pieces, position, 0, keepdims=False)
        spread = jnp.where(at_depth, piece[:, None], jnp.zeros((), jnp.bfloat16))
        source = lax.dot_general(
            spread, at_plane, (((0,), (0,)), ((), ())), preferred_element_type=jnp.float32
        ).T.reshape(current.shape)
        following = 2.0 * current - before + courant * (
            laplace(current, x_lo, x_hi, y_lo, y_hi) + source
        )
        snapshot = lax.dynamic_index_in_dim(forward_field, position, 0, keepdims=False)
        imaging = imaging + snapshot.astype(jnp.float32) * following
        return (following, current, imaging)

    current, before, imaging = lax.fori_loop(
        0, STEPS, advance, (adjoint_now, adjoint_prev, image_start)
    )
    return (current, before, imaging)


def solution(mesh):
    return jax.shard_map(
        per_device,
        mesh=mesh,
        in_specs=(
            P(None, ("gx", "gy")),
            P(None, ("gx", "gy")),
            P(),
            P(("gx", "gy")),
            P(("gx", "gy"), None),
            P(("gx", "gy")),
            P("gx", "gy", None),
            P("gx", "gy", None),
            P("gx", "gy", None),
            P(None, "gx", "gy", None),
            P("gx", "gy", None),
        ),
        out_specs=(P("gx", "gy", None), P("gx", "gy", None), P("gx", "gy", None)),
        check_vma=False,
    )
```

```python
import functools

import jax
import jax.numpy as jnp
from jax import lax
from jax.experimental import pallas as pl
from jax.experimental.pallas import tpu as pltpu
from jax.sharding import PartitionSpec as P

MESH = pl.DeviceIdType.MESH

STEPS = 16
SHOTS = 16
TAPS = 17
HALO = 4


stencil_weights = (-205.0 / 72.0, 8.0 / 5.0, -1.0 / 5.0, 8.0 / 315.0, -1.0 / 560.0)


def faces(value, axis, dim):
    peers, length = lax.axis_size(axis), value.shape[dim]
    up = [(i, i + 1) for i in range(peers - 1)]
    down = [(j, i) for i, j in up]
    last = lax.slice_in_dim(value, length - HALO, length, axis=dim)
    first = lax.slice_in_dim(value, 0, HALO, axis=dim)
    return lax.ppermute(last, axis, up), lax.ppermute(first, axis, down)


def step_kernel(
    grid_x, grid_y, cur_ref, prev_ref, courant_ref, snap_ref, image_ref, source_ref,
    next_ref, image_out_ref, ext_x, ext_y, send_sem, recv_sem, local_sem,
):
    me_x = lax.axis_index("gx")
    me_y = lax.axis_index("gy")
    width_x, width_y, column = cur_ref.shape
    has = (me_x > 0, me_x < grid_x - 1, me_y > 0, me_y < grid_y - 1)
    peers = ((me_x - 1, me_y), (me_x + 1, me_y), (me_x, me_y - 1), (me_x, me_y + 1))
    count = sum(flag.astype(jnp.int32) for flag in has)

    center_x = pltpu.make_async_copy(cur_ref, ext_x.at[pl.ds(HALO, width_x)], local_sem.at[0])
    center_y = pltpu.make_async_copy(cur_ref, ext_y.at[:, pl.ds(2 * HALO, width_y)], local_sem.at[1])
    center_x.start()
    center_y.start()

    barrier = pltpu.get_barrier_semaphore()
    for flag, peer in zip(has, peers):
        @pl.when(flag)
        def _():
            pl.semaphore_signal(barrier, inc=1, device_id=peer, device_id_type=MESH)
    pl.semaphore_wait(barrier, count)

    zones = (
        ext_x.at[pl.ds(0, HALO)],
        ext_x.at[pl.ds(HALO + width_x, HALO)],
        ext_y.at[:, pl.ds(HALO, HALO)],
        ext_y.at[:, pl.ds(2 * HALO + width_y, HALO)],
    )
    faces = (
        cur_ref.at[pl.ds(0, HALO)],
        cur_ref.at[pl.ds(width_x - HALO, HALO)],
        cur_ref.at[:, pl.ds(0, HALO)],
        cur_ref.at[:, pl.ds(width_y - HALO, HALO)],
    )
    zone_of = (1, 0, 3, 2)

    def copy_to(side):
        zone = zone_of[side]
        return pltpu.make_async_remote_copy(
            src_ref=faces[side],
            dst_ref=zones[zone],
            send_sem=send_sem.at[side],
            recv_sem=recv_sem.at[zone],
            device_id=peers[side],
            device_id_type=MESH,
        )

    for side in range(4):
        @pl.when(has[side])
        def _():
            copy_to(side).start()

    arriving = (copy_to(1), copy_to(0), copy_to(3), copy_to(2))
    for zone in range(4):
        @pl.when(has[zone])
        def _():
            arriving[zone].wait_recv()

        @pl.when(jnp.logical_not(has[zone]))
        def _():
            zones[zone][...] = jnp.zeros(zones[zone].shape, jnp.float32)

    center_x.wait()
    center_y.wait()

    lane = lax.broadcasted_iota(jnp.int32, (width_y, column), 1)

    def row(x, carry):
        center = ext_x[x + HALO]
        summed = 3.0 * stencil_weights[0] * center
        for offset in range(1, 5):
            along_x = ext_x[x + HALO + offset] + ext_x[x + HALO - offset]
            along_y = (
                ext_y[x, pl.ds(2 * HALO + offset, width_y), :]
                + ext_y[x, pl.ds(2 * HALO - offset, width_y), :]
            )
            above = jnp.where(lane < column - offset, pltpu.roll(center, column - offset, 1), 0.0)
            below = jnp.where(lane >= offset, pltpu.roll(center, offset, 1), 0.0)
            summed = summed + stencil_weights[offset] * (along_x + along_y + (above + below))
        following = 2.0 * center - prev_ref[x] + courant_ref[x] * (summed + source_ref[x])
        next_ref[x] = following
        image_out_ref[x] = image_ref[x] + snap_ref[x].astype(jnp.float32) * following
        return carry

    lax.fori_loop(0, width_x, row, 0)

    for side in range(4):
        @pl.when(has[side])
        def _():
            copy_to(side).wait_send()


def fused_step(current, before, courant, snapshot, imaging, source):
    grid_x, grid_y = lax.axis_size("gx"), lax.axis_size("gy")
    width_x, width_y, column = current.shape
    field = jax.ShapeDtypeStruct(current.shape, jnp.float32)
    vmem = pl.BlockSpec(memory_space=pltpu.VMEM)
    return pl.pallas_call(
        functools.partial(step_kernel, grid_x, grid_y),
        out_shape=(field, field),
        in_specs=[vmem] * 6,
        out_specs=(vmem, vmem),
        scratch_shapes=[
            pltpu.VMEM((width_x + 2 * HALO, width_y, column), jnp.float32),
            pltpu.VMEM((width_x, width_y + 4 * HALO, column), jnp.float32),
            pltpu.SemaphoreType.DMA((4,)),
            pltpu.SemaphoreType.DMA((4,)),
            pltpu.SemaphoreType.DMA((2,)),
        ],
        compiler_params=pltpu.CompilerParams(
            collective_id=0, has_side_effects=True, vmem_limit_bytes=48 * 1024 * 1024
        ),
    )(current, before, courant, snapshot, imaging, source)


def split_high(value):
    scaled = value * 65537.0
    return scaled - (scaled - value)


def laplace(center, x_lo, x_hi, y_lo, y_hi):
    width_x, width_y, column = center.shape
    along_x_src = jnp.concatenate([x_lo, center, x_hi], axis=0)
    along_y_src = jnp.concatenate([y_lo, center, y_hi], axis=1)
    z_padded = jnp.pad(center, ((0, 0), (0, 0), (4, 4)))
    summed = 3.0 * stencil_weights[0] * center
    for offset in range(1, 5):
        along_x = (
            along_x_src[4 + offset : 4 + offset + width_x]
            + along_x_src[4 - offset : 4 - offset + width_x]
        )
        along_y = (
            along_y_src[:, 4 + offset : 4 + offset + width_y]
            + along_y_src[:, 4 - offset : 4 - offset + width_y]
        )
        along_z = (
            z_padded[:, :, 4 + offset : 4 + offset + column]
            + z_padded[:, :, 4 - offset : 4 - offset + column]
        )
        summed = summed + stencil_weights[offset] * (along_x + along_y + along_z)
    return summed


def per_device(
    observed,
    synthetic,
    match_filter,
    trace_shot,
    trace_owner,
    trace_cell,
    courant,
    adjoint_now,
    adjoint_prev,
    forward_field,
    image_start,
):
    trace_rows = observed.shape[1]
    grid_x = lax.axis_size("gx")
    grid_y = lax.axis_size("gy")
    devices = grid_x * grid_y
    capacity = max(2, 2 * trace_rows // devices)
    slot_count = devices * capacity
    shot_match = (trace_shot[:, None] == jnp.arange(SHOTS, dtype=jnp.int32)[None, :]).astype(
        jnp.float32
    )
    filters = jnp.dot(match_filter.T, shot_match.T, precision=lax.Precision.HIGHEST)
    residual = -observed
    for lag_index in range(TAPS):
        residual = (
            residual
            + filters[lag_index][None, :] * synthetic[STEPS - lag_index : 2 * STEPS - lag_index]
        )
    owners = trace_owner[:, 0]
    same_owner = owners[:, None] == owners[None, :]
    row_ids = jnp.arange(trace_rows, dtype=jnp.int32)
    earlier = row_ids[None, :] < row_ids[:, None]
    ranks = jnp.sum((same_owner & earlier).astype(jnp.int32), axis=1)
    slot_index = owners * capacity + ranks
    slot_table = (slot_index[:, None] == jnp.arange(slot_count, dtype=jnp.int32)[None, :]).astype(
        jnp.float32
    )
    payload = jnp.concatenate([residual, trace_cell.astype(jnp.float32)[None, :]], axis=0)
    parcel = jnp.dot(payload, slot_table, precision=lax.Precision.HIGHEST)
    received = lax.all_to_all(parcel, ("gx", "gy"), split_axis=1, concat_axis=1, tiled=True)
    got_values = received[:STEPS][::-1]
    got_cells = received[STEPS].astype(jnp.int32)
    plane = courant.shape[0] * courant.shape[1]
    column = courant.shape[2]
    got_plane = got_cells // column
    got_depth = got_cells % column
    at_plane = (got_plane[:, None] == jnp.arange(plane, dtype=jnp.int32)[None, :]).astype(jnp.bfloat16)
    at_plane = jnp.concatenate([at_plane] * 3, axis=0)
    at_depth = got_depth[:, None] == jnp.arange(column, dtype=jnp.int32)[None, :]
    at_depth = jnp.concatenate([at_depth] * 3, axis=0)
    top = split_high(got_values)
    rest = got_values - top
    second = split_high(rest)
    pieces = jnp.concatenate([top, second, rest - second], axis=1).astype(jnp.bfloat16)

    def advance(position, carry):
        current, before, imaging = carry
        piece = lax.dynamic_index_in_dim(pieces, position, 0, keepdims=False)
        spread = jnp.where(at_depth, piece[:, None], jnp.zeros((), jnp.bfloat16))
        source = lax.dot_general(
            spread, at_plane, (((0,), (0,)), ((), ())), preferred_element_type=jnp.float32
        ).T.reshape(current.shape)
        snapshot = lax.dynamic_index_in_dim(forward_field, position, 0, keepdims=False)
        following, imaging = fused_step(current, before, courant, snapshot, imaging, source)
        return (following, current, imaging)

    current, before, imaging = lax.fori_loop(
        0, STEPS, advance, (adjoint_now, adjoint_prev, image_start)
    )
    return (current, before, imaging)


def solution(mesh):
    return jax.shard_map(
        per_device,
        mesh=mesh,
        in_specs=(
            P(None, ("gx", "gy")),
            P(None, ("gx", "gy")),
            P(),
            P(("gx", "gy")),
            P(("gx", "gy"), None),
            P(("gx", "gy")),
            P("gx", "gy", None),
            P("gx", "gy", None),
            P("gx", "gy", None),
            P(None, "gx", "gy", None),
            P("gx", "gy", None),
        ),
        out_specs=(P("gx", "gy", None), P("gx", "gy", None), P("gx", "gy", None)),
        check_vma=False,
    )
```

```python
import functools

import jax
import jax.numpy as jnp
from jax import lax
from jax.experimental import pallas as pl
from jax.experimental.pallas import tpu as pltpu
from jax.sharding import PartitionSpec as P

MESH = pl.DeviceIdType.MESH

STEPS = 16
SHOTS = 16
TAPS = 17
HALO = 4


stencil_weights = (-205.0 / 72.0, 8.0 / 5.0, -1.0 / 5.0, 8.0 / 315.0, -1.0 / 560.0)


def faces(value, axis, dim):
    peers, length = lax.axis_size(axis), value.shape[dim]
    up = [(i, i + 1) for i in range(peers - 1)]
    down = [(j, i) for i, j in up]
    last = lax.slice_in_dim(value, length - HALO, length, axis=dim)
    first = lax.slice_in_dim(value, 0, HALO, axis=dim)
    return lax.ppermute(last, axis, up), lax.ppermute(first, axis, down)


def step_kernel(
    grid_x, grid_y, cur_ref, prev_ref, courant_ref, snap_ref, image_ref, plane_ref, spread_ref,
    next_ref, image_out_ref, ext_x, ext_y, source_ref, send_sem, recv_sem, local_sem,
):
    me_x = lax.axis_index("gx")
    me_y = lax.axis_index("gy")
    width_x, width_y, column = cur_ref.shape
    has = (me_x > 0, me_x < grid_x - 1, me_y > 0, me_y < grid_y - 1)
    peers = ((me_x - 1, me_y), (me_x + 1, me_y), (me_x, me_y - 1), (me_x, me_y + 1))
    count = sum(flag.astype(jnp.int32) for flag in has)

    center_x = pltpu.make_async_copy(cur_ref, ext_x.at[pl.ds(HALO, width_x)], local_sem.at[0])
    center_y = pltpu.make_async_copy(cur_ref, ext_y.at[:, pl.ds(2 * HALO, width_y)], local_sem.at[1])
    center_x.start()
    center_y.start()

    barrier = pltpu.get_barrier_semaphore()
    for flag, peer in zip(has, peers):
        @pl.when(flag)
        def _():
            pl.semaphore_signal(barrier, inc=1, device_id=peer, device_id_type=MESH)
    pl.semaphore_wait(barrier, count)

    zones = (
        ext_x.at[pl.ds(0, HALO)],
        ext_x.at[pl.ds(HALO + width_x, HALO)],
        ext_y.at[:, pl.ds(HALO, HALO)],
        ext_y.at[:, pl.ds(2 * HALO + width_y, HALO)],
    )
    faces = (
        cur_ref.at[pl.ds(0, HALO)],
        cur_ref.at[pl.ds(width_x - HALO, HALO)],
        cur_ref.at[:, pl.ds(0, HALO)],
        cur_ref.at[:, pl.ds(width_y - HALO, HALO)],
    )
    zone_of = (1, 0, 3, 2)

    def copy_to(side):
        zone = zone_of[side]
        return pltpu.make_async_remote_copy(
            src_ref=faces[side],
            dst_ref=zones[zone],
            send_sem=send_sem.at[side],
            recv_sem=recv_sem.at[zone],
            device_id=peers[side],
            device_id_type=MESH,
        )

    for side in range(4):
        @pl.when(has[side])
        def _():
            copy_to(side).start()

    source_ref[...] = jnp.dot(plane_ref[...], spread_ref[...], preferred_element_type=jnp.float32)

    arriving = (copy_to(1), copy_to(0), copy_to(3), copy_to(2))
    for zone in range(4):
        @pl.when(has[zone])
        def _():
            arriving[zone].wait_recv()

        @pl.when(jnp.logical_not(has[zone]))
        def _():
            zones[zone][...] = jnp.zeros(zones[zone].shape, jnp.float32)

    center_x.wait()
    center_y.wait()

    lane = lax.broadcasted_iota(jnp.int32, (width_y, column), 1)

    def row(x, carry):
        center = ext_x[x + HALO]
        summed = 3.0 * stencil_weights[0] * center
        for offset in range(1, 5):
            along_x = ext_x[x + HALO + offset] + ext_x[x + HALO - offset]
            along_y = (
                ext_y[x, pl.ds(2 * HALO + offset, width_y), :]
                + ext_y[x, pl.ds(2 * HALO - offset, width_y), :]
            )
            above = jnp.where(lane < column - offset, pltpu.roll(center, column - offset, 1), 0.0)
            below = jnp.where(lane >= offset, pltpu.roll(center, offset, 1), 0.0)
            summed = summed + stencil_weights[offset] * (along_x + along_y + (above + below))
        rows = pl.ds(pl.multiple_of(x * width_y, width_y), width_y)
        source = (
            source_ref[rows, pl.ds(0, column)] + source_ref[rows, pl.ds(column, column)]
        ) + source_ref[rows, pl.ds(2 * column, column)]
        following = 2.0 * center - prev_ref[x] + courant_ref[x] * (summed + source)
        next_ref[x] = following
        image_out_ref[x] = image_ref[x] + snap_ref[x].astype(jnp.float32) * following
        return carry

    lax.fori_loop(0, width_x, row, 0)

    for side in range(4):
        @pl.when(has[side])
        def _():
            copy_to(side).wait_send()


def fused_step(current, before, courant, snapshot, imaging, at_plane, spread):
    grid_x, grid_y = lax.axis_size("gx"), lax.axis_size("gy")
    width_x, width_y, column = current.shape
    field = jax.ShapeDtypeStruct(current.shape, jnp.float32)
    vmem = pl.BlockSpec(memory_space=pltpu.VMEM)
    return pl.pallas_call(
        functools.partial(step_kernel, grid_x, grid_y),
        out_shape=(field, field),
        in_specs=[vmem] * 7,
        out_specs=(vmem, vmem),
        scratch_shapes=[
            pltpu.VMEM((width_x + 2 * HALO, width_y, column), jnp.float32),
            pltpu.VMEM((width_x, width_y + 4 * HALO, column), jnp.float32),
            pltpu.VMEM((width_x * width_y, 3 * column), jnp.float32),
            pltpu.SemaphoreType.DMA((4,)),
            pltpu.SemaphoreType.DMA((4,)),
            pltpu.SemaphoreType.DMA((2,)),
        ],
        compiler_params=pltpu.CompilerParams(
            collective_id=0, has_side_effects=True, vmem_limit_bytes=48 * 1024 * 1024
        ),
    )(current, before, courant, snapshot, imaging, at_plane, spread)


def split_high(value):
    scaled = value * 65537.0
    return scaled - (scaled - value)


def laplace(center, x_lo, x_hi, y_lo, y_hi):
    width_x, width_y, column = center.shape
    along_x_src = jnp.concatenate([x_lo, center, x_hi], axis=0)
    along_y_src = jnp.concatenate([y_lo, center, y_hi], axis=1)
    z_padded = jnp.pad(center, ((0, 0), (0, 0), (4, 4)))
    summed = 3.0 * stencil_weights[0] * center
    for offset in range(1, 5):
        along_x = (
            along_x_src[4 + offset : 4 + offset + width_x]
            + along_x_src[4 - offset : 4 - offset + width_x]
        )
        along_y = (
            along_y_src[:, 4 + offset : 4 + offset + width_y]
            + along_y_src[:, 4 - offset : 4 - offset + width_y]
        )
        along_z = (
            z_padded[:, :, 4 + offset : 4 + offset + column]
            + z_padded[:, :, 4 - offset : 4 - offset + column]
        )
        summed = summed + stencil_weights[offset] * (along_x + along_y + along_z)
    return summed


def per_device(
    observed,
    synthetic,
    match_filter,
    trace_shot,
    trace_owner,
    trace_cell,
    courant,
    adjoint_now,
    adjoint_prev,
    forward_field,
    image_start,
):
    trace_rows = observed.shape[1]
    grid_x = lax.axis_size("gx")
    grid_y = lax.axis_size("gy")
    devices = grid_x * grid_y
    capacity = max(2, 2 * trace_rows // devices)
    slot_count = devices * capacity
    shot_match = (trace_shot[:, None] == jnp.arange(SHOTS, dtype=jnp.int32)[None, :]).astype(
        jnp.float32
    )
    filters = jnp.dot(match_filter.T, shot_match.T, precision=lax.Precision.HIGHEST)
    residual = -observed
    for lag_index in range(TAPS):
        residual = (
            residual
            + filters[lag_index][None, :] * synthetic[STEPS - lag_index : 2 * STEPS - lag_index]
        )
    owners = trace_owner[:, 0]
    same_owner = owners[:, None] == owners[None, :]
    row_ids = jnp.arange(trace_rows, dtype=jnp.int32)
    earlier = row_ids[None, :] < row_ids[:, None]
    ranks = jnp.sum((same_owner & earlier).astype(jnp.int32), axis=1)
    slot_index = owners * capacity + ranks
    slot_table = (slot_index[:, None] == jnp.arange(slot_count, dtype=jnp.int32)[None, :]).astype(
        jnp.float32
    )
    payload = jnp.concatenate([residual, trace_cell.astype(jnp.float32)[None, :]], axis=0)
    parcel = jnp.dot(payload, slot_table, precision=lax.Precision.HIGHEST)
    received = lax.all_to_all(parcel, ("gx", "gy"), split_axis=1, concat_axis=1, tiled=True)
    got_values = received[:STEPS][::-1]
    got_cells = received[STEPS].astype(jnp.int32)
    plane = courant.shape[0] * courant.shape[1]
    column = courant.shape[2]
    got_plane = got_cells // column
    got_depth = got_cells % column
    at_plane = (got_plane[None, :] == jnp.arange(plane, dtype=jnp.int32)[:, None]).astype(jnp.bfloat16)
    at_depth = got_depth[:, None] == jnp.arange(column, dtype=jnp.int32)[None, :]
    top = split_high(got_values)
    rest = got_values - top
    second = split_high(rest)
    pieces = jnp.stack([top, second, rest - second], axis=2).astype(jnp.bfloat16)

    def advance(position, carry):
        current, before, imaging = carry
        piece = lax.dynamic_index_in_dim(pieces, position, 0, keepdims=False)
        spread = jnp.where(
            at_depth[:, None, :], piece[:, :, None], jnp.zeros((), jnp.bfloat16)
        ).reshape(piece.shape[0], 3 * column)
        snapshot = lax.dynamic_index_in_dim(forward_field, position, 0, keepdims=False)
        following, imaging = fused_step(
            current, before, courant, snapshot, imaging, at_plane, spread
        )
        return (following, current, imaging)

    current, before, imaging = lax.fori_loop(
        0, STEPS, advance, (adjoint_now, adjoint_prev, image_start)
    )
    return (current, before, imaging)


def solution(mesh):
    return jax.shard_map(
        per_device,
        mesh=mesh,
        in_specs=(
            P(None, ("gx", "gy")),
            P(None, ("gx", "gy")),
            P(),
            P(("gx", "gy")),
            P(("gx", "gy"), None),
            P(("gx", "gy")),
            P("gx", "gy", None),
            P("gx", "gy", None),
            P("gx", "gy", None),
            P(None, "gx", "gy", None),
            P("gx", "gy", None),
        ),
        out_specs=(P("gx", "gy", None), P("gx", "gy", None), P("gx", "gy", None)),
        check_vma=False,
    )
```

```python
import functools

import jax
import jax.numpy as jnp
from jax import lax
from jax.experimental import pallas as pl
from jax.experimental.pallas import tpu as pltpu
from jax.sharding import PartitionSpec as P

MESH = pl.DeviceIdType.MESH

STEPS = 16
SHOTS = 16
TAPS = 17
HALO = 4


stencil_weights = (-205.0 / 72.0, 8.0 / 5.0, -1.0 / 5.0, 8.0 / 315.0, -1.0 / 560.0)


def faces(value, axis, dim):
    peers, length = lax.axis_size(axis), value.shape[dim]
    up = [(i, i + 1) for i in range(peers - 1)]
    down = [(j, i) for i, j in up]
    last = lax.slice_in_dim(value, length - HALO, length, axis=dim)
    first = lax.slice_in_dim(value, 0, HALO, axis=dim)
    return lax.ppermute(last, axis, up), lax.ppermute(first, axis, down)


def window_kernel(
    grid_x, grid_y, now_ref, prev_ref, courant_ref, image_ref, plane_ref, snaps_hbm, spreads_hbm,
    field_ref, before_ref, image_out_ref,
    ext_x, ext_y, source_ref, spread_buf, snap_buf, send_sem, recv_sem, local_sem,
):
    me_x = lax.axis_index("gx")
    me_y = lax.axis_index("gy")
    width_x, width_y, column = now_ref.shape
    steps = snaps_hbm.shape[0]
    has = (me_x > 0, me_x < grid_x - 1, me_y > 0, me_y < grid_y - 1)
    peers = ((me_x - 1, me_y), (me_x + 1, me_y), (me_x, me_y - 1), (me_x, me_y + 1))
    count = sum(flag.astype(jnp.int32) for flag in has)
    mid_x = pl.ds(HALO, width_x)
    mid_y = pl.ds(2 * HALO, width_y)

    starts = (
        pltpu.make_async_copy(now_ref, ext_x.at[0, mid_x], local_sem.at[0]),
        pltpu.make_async_copy(now_ref, ext_y.at[0, :, mid_y], local_sem.at[1]),
        pltpu.make_async_copy(prev_ref, ext_x.at[2, mid_x], local_sem.at[2]),
        pltpu.make_async_copy(image_ref, image_out_ref, local_sem.at[3]),
    )
    for copy in starts:
        copy.start()

    def zones(slot):
        return (
            ext_x.at[slot, pl.ds(0, HALO)],
            ext_x.at[slot, pl.ds(HALO + width_x, HALO)],
            ext_y.at[slot, :, pl.ds(HALO, HALO)],
            ext_y.at[slot, :, pl.ds(2 * HALO + width_y, HALO)],
        )

    for slot in range(3):
        for zone in range(4):
            @pl.when(jnp.logical_not(has[zone]))
            def _():
                target = zones(slot)[zone]
                target[...] = jnp.zeros(target.shape, jnp.float32)

    for copy in starts:
        copy.wait()

    barrier = pltpu.get_barrier_semaphore()
    for flag, peer in zip(has, peers):
        @pl.when(flag)
        def _():
            pl.semaphore_signal(barrier, inc=1, device_id=peer, device_id_type=MESH)
    pl.semaphore_wait(barrier, count)

    zone_of = (1, 0, 3, 2)
    lane = lax.broadcasted_iota(jnp.int32, (width_y, column), 1)

    def copy_to(slot, side):
        faces = (
            ext_x.at[slot, pl.ds(HALO, HALO)],
            ext_x.at[slot, pl.ds(width_x, HALO)],
            ext_y.at[slot, :, pl.ds(2 * HALO, HALO)],
            ext_y.at[slot, :, pl.ds(HALO + width_y, HALO)],
        )
        zone = zone_of[side]
        return pltpu.make_async_remote_copy(
            src_ref=faces[side],
            dst_ref=zones(slot)[zone],
            send_sem=send_sem.at[side],
            recv_sem=recv_sem.at[slot, zone],
            device_id=peers[side],
            device_id_type=MESH,
        )

    def step(position, carry):
        now = position % 3
        after = (position + 1) % 3
        last = (position + 2) % 3
        spread_in = pltpu.make_async_copy(spreads_hbm.at[position], spread_buf, local_sem.at[4])
        snap_in = pltpu.make_async_copy(snaps_hbm.at[position], snap_buf, local_sem.at[5])
        spread_in.start()
        snap_in.start()
        for side in range(4):
            @pl.when(has[side])
            def _():
                copy_to(now, side).start()

        spread_in.wait()
        source_ref[...] = jnp.dot(plane_ref[...], spread_buf[...], preferred_element_type=jnp.float32)

        for zone, side in enumerate(zone_of):
            @pl.when(has[zone])
            def _():
                copy_to(now, side).wait_recv()
        snap_in.wait()

        def row(x, inner):
            center = ext_x[now, x + HALO]
            summed = 3.0 * stencil_weights[0] * center
            for offset in range(1, 5):
                along_x = ext_x[now, x + HALO + offset] + ext_x[now, x + HALO - offset]
                along_y = (
                    ext_y[now, x, pl.ds(2 * HALO + offset, width_y), :]
                    + ext_y[now, x, pl.ds(2 * HALO - offset, width_y), :]
                )
                above = jnp.where(lane < column - offset, pltpu.roll(center, column - offset, 1), 0.0)
                below = jnp.where(lane >= offset, pltpu.roll(center, offset, 1), 0.0)
                summed = summed + stencil_weights[offset] * (along_x + along_y + (above + below))
            rows = pl.ds(pl.multiple_of(x * width_y, width_y), width_y)
            source = (
                source_ref[rows, pl.ds(0, column)] + source_ref[rows, pl.ds(column, column)]
            ) + source_ref[rows, pl.ds(2 * column, column)]
            following = 2.0 * center - ext_x[last, x + HALO] + courant_ref[x] * (summed + source)
            ext_x[after, x + HALO] = following
            ext_y[after, x, mid_y, :] = following
            image_out_ref[x] = image_out_ref[x] + snap_buf[x].astype(jnp.float32) * following
            return inner

        lax.fori_loop(0, width_x, row, 0)

        for side in range(4):
            @pl.when(has[side])
            def _():
                copy_to(now, side).wait_send()
        return carry

    lax.fori_loop(0, steps, step, 0)

    ends = (
        pltpu.make_async_copy(ext_x.at[steps % 3, mid_x], field_ref, local_sem.at[0]),
        pltpu.make_async_copy(ext_x.at[(steps - 1) % 3, mid_x], before_ref, local_sem.at[1]),
    )
    for copy in ends:
        copy.start()
    for copy in ends:
        copy.wait()


def whole_window(now, before, courant, imaging, at_plane, snaps, spreads):
    grid_x, grid_y = lax.axis_size("gx"), lax.axis_size("gy")
    width_x, width_y, column = now.shape
    field = jax.ShapeDtypeStruct(now.shape, jnp.float32)
    vmem = pl.BlockSpec(memory_space=pltpu.VMEM)
    hbm = pl.BlockSpec(memory_space=pl.ANY)
    return pl.pallas_call(
        functools.partial(window_kernel, grid_x, grid_y),
        out_shape=(field, field, field),
        in_specs=[vmem] * 5 + [hbm, hbm],
        out_specs=(vmem, vmem, vmem),
        scratch_shapes=[
            pltpu.VMEM((3, width_x + 2 * HALO, width_y, column), jnp.float32),
            pltpu.VMEM((3, width_x, width_y + 4 * HALO, column), jnp.float32),
            pltpu.VMEM((width_x * width_y, 3 * column), jnp.float32),
            pltpu.VMEM(spreads.shape[1:], spreads.dtype),
            pltpu.VMEM(snaps.shape[1:], snaps.dtype),
            pltpu.SemaphoreType.DMA((4,)),
            pltpu.SemaphoreType.DMA((3, 4)),
            pltpu.SemaphoreType.DMA((6,)),
        ],
        compiler_params=pltpu.CompilerParams(
            collective_id=0, has_side_effects=True, vmem_limit_bytes=60 * 1024 * 1024
        ),
    )(now, before, courant, imaging, at_plane, snaps, spreads)


def split_high(value):
    scaled = value * 65537.0
    return scaled - (scaled - value)


def laplace(center, x_lo, x_hi, y_lo, y_hi):
    width_x, width_y, column = center.shape
    along_x_src = jnp.concatenate([x_lo, center, x_hi], axis=0)
    along_y_src = jnp.concatenate([y_lo, center, y_hi], axis=1)
    z_padded = jnp.pad(center, ((0, 0), (0, 0), (4, 4)))
    summed = 3.0 * stencil_weights[0] * center
    for offset in range(1, 5):
        along_x = (
            along_x_src[4 + offset : 4 + offset + width_x]
            + along_x_src[4 - offset : 4 - offset + width_x]
        )
        along_y = (
            along_y_src[:, 4 + offset : 4 + offset + width_y]
            + along_y_src[:, 4 - offset : 4 - offset + width_y]
        )
        along_z = (
            z_padded[:, :, 4 + offset : 4 + offset + column]
            + z_padded[:, :, 4 - offset : 4 - offset + column]
        )
        summed = summed + stencil_weights[offset] * (along_x + along_y + along_z)
    return summed


def per_device(
    observed,
    synthetic,
    match_filter,
    trace_shot,
    trace_owner,
    trace_cell,
    courant,
    adjoint_now,
    adjoint_prev,
    forward_field,
    image_start,
):
    trace_rows = observed.shape[1]
    grid_x = lax.axis_size("gx")
    grid_y = lax.axis_size("gy")
    devices = grid_x * grid_y
    capacity = max(2, 2 * trace_rows // devices)
    slot_count = devices * capacity
    shot_match = (trace_shot[:, None] == jnp.arange(SHOTS, dtype=jnp.int32)[None, :]).astype(
        jnp.float32
    )
    filters = jnp.dot(match_filter.T, shot_match.T, precision=lax.Precision.HIGHEST)
    residual = -observed
    for lag_index in range(TAPS):
        residual = (
            residual
            + filters[lag_index][None, :] * synthetic[STEPS - lag_index : 2 * STEPS - lag_index]
        )
    owners = trace_owner[:, 0]
    same_owner = owners[:, None] == owners[None, :]
    row_ids = jnp.arange(trace_rows, dtype=jnp.int32)
    earlier = row_ids[None, :] < row_ids[:, None]
    ranks = jnp.sum((same_owner & earlier).astype(jnp.int32), axis=1)
    slot_index = owners * capacity + ranks
    slot_table = (slot_index[:, None] == jnp.arange(slot_count, dtype=jnp.int32)[None, :]).astype(
        jnp.float32
    )
    payload = jnp.concatenate([residual, trace_cell.astype(jnp.float32)[None, :]], axis=0)
    parcel = jnp.dot(payload, slot_table, precision=lax.Precision.HIGHEST)
    received = lax.all_to_all(parcel, ("gx", "gy"), split_axis=1, concat_axis=1, tiled=True)
    got_values = received[:STEPS][::-1]
    got_cells = received[STEPS].astype(jnp.int32)
    plane = courant.shape[0] * courant.shape[1]
    column = courant.shape[2]
    got_plane = got_cells // column
    got_depth = got_cells % column
    at_plane = (got_plane[None, :] == jnp.arange(plane, dtype=jnp.int32)[:, None]).astype(jnp.bfloat16)
    at_depth = got_depth[:, None] == jnp.arange(column, dtype=jnp.int32)[None, :]
    top = split_high(got_values)
    rest = got_values - top
    second = split_high(rest)
    pieces = jnp.stack([top, second, rest - second], axis=2).astype(jnp.bfloat16)

    spreads = jnp.where(
        at_depth[None, :, None, :], pieces[:, :, :, None], jnp.zeros((), jnp.bfloat16)
    ).reshape(pieces.shape[0], pieces.shape[1], 3 * column)
    current, before, imaging = whole_window(
        adjoint_now, adjoint_prev, courant, image_start, at_plane, forward_field, spreads
    )
    return (current, before, imaging)


def solution(mesh):
    return jax.shard_map(
        per_device,
        mesh=mesh,
        in_specs=(
            P(None, ("gx", "gy")),
            P(None, ("gx", "gy")),
            P(),
            P(("gx", "gy")),
            P(("gx", "gy"), None),
            P(("gx", "gy")),
            P("gx", "gy", None),
            P("gx", "gy", None),
            P("gx", "gy", None),
            P(None, "gx", "gy", None),
            P("gx", "gy", None),
        ),
        out_specs=(P("gx", "gy", None), P("gx", "gy", None), P("gx", "gy", None)),
        check_vma=False,
    )
```

```python
import functools

import jax
import jax.numpy as jnp
from jax import lax
from jax.experimental import pallas as pl
from jax.experimental.pallas import tpu as pltpu
from jax.sharding import PartitionSpec as P

MESH = pl.DeviceIdType.MESH

STEPS = 16
SHOTS = 16
TAPS = 17
HALO = 4


stencil_weights = (-205.0 / 72.0, 8.0 / 5.0, -1.0 / 5.0, 8.0 / 315.0, -1.0 / 560.0)


def faces(value, axis, dim):
    peers, length = lax.axis_size(axis), value.shape[dim]
    up = [(i, i + 1) for i in range(peers - 1)]
    down = [(j, i) for i, j in up]
    last = lax.slice_in_dim(value, length - HALO, length, axis=dim)
    first = lax.slice_in_dim(value, 0, HALO, axis=dim)
    return lax.ppermute(last, axis, up), lax.ppermute(first, axis, down)


def window_kernel(
    grid_x, grid_y, now_ref, prev_ref, courant_ref, image_ref, plane_ref, snaps_hbm, spreads_hbm,
    field_ref, before_ref, image_out_ref,
    ext_x, ext_y, source_ref, spread_buf, snap_buf, send_sem, recv_sem, local_sem,
):
    me_x = lax.axis_index("gx")
    me_y = lax.axis_index("gy")
    width_x, width_y, column = now_ref.shape
    steps = snaps_hbm.shape[0]
    has = (me_x > 0, me_x < grid_x - 1, me_y > 0, me_y < grid_y - 1)
    peers = ((me_x - 1, me_y), (me_x + 1, me_y), (me_x, me_y - 1), (me_x, me_y + 1))
    count = sum(flag.astype(jnp.int32) for flag in has)
    mid_x = pl.ds(HALO, width_x)
    mid_y = pl.ds(2 * HALO, width_y)

    starts = (
        pltpu.make_async_copy(now_ref, ext_x.at[0, mid_x], local_sem.at[0]),
        pltpu.make_async_copy(now_ref, ext_y.at[0, :, mid_y], local_sem.at[1]),
        pltpu.make_async_copy(prev_ref, ext_x.at[2, mid_x], local_sem.at[2]),
        pltpu.make_async_copy(image_ref, image_out_ref, local_sem.at[3]),
    )
    for copy in starts:
        copy.start()

    def zones(slot):
        return (
            ext_x.at[slot, pl.ds(0, HALO)],
            ext_x.at[slot, pl.ds(HALO + width_x, HALO)],
            ext_y.at[slot, :, pl.ds(HALO, HALO)],
            ext_y.at[slot, :, pl.ds(2 * HALO + width_y, HALO)],
        )

    for slot in range(3):
        for zone in range(4):
            @pl.when(jnp.logical_not(has[zone]))
            def _():
                target = zones(slot)[zone]
                target[...] = jnp.zeros(target.shape, jnp.float32)

    for copy in starts:
        copy.wait()

    barrier = pltpu.get_barrier_semaphore()
    for flag, peer in zip(has, peers):
        @pl.when(flag)
        def _():
            pl.semaphore_signal(barrier, inc=1, device_id=peer, device_id_type=MESH)
    pl.semaphore_wait(barrier, count)

    zone_of = (1, 0, 3, 2)
    lane = lax.broadcasted_iota(jnp.int32, (width_y, column), 1)

    def copy_to(slot, side):
        faces = (
            ext_x.at[slot, pl.ds(HALO, HALO)],
            ext_x.at[slot, pl.ds(width_x, HALO)],
            ext_y.at[slot, :, pl.ds(2 * HALO, HALO)],
            ext_y.at[slot, :, pl.ds(HALO + width_y, HALO)],
        )
        zone = zone_of[side]
        return pltpu.make_async_remote_copy(
            src_ref=faces[side],
            dst_ref=zones(slot)[zone],
            send_sem=send_sem.at[side],
            recv_sem=recv_sem.at[slot, zone],
            device_id=peers[side],
            device_id_type=MESH,
        )

    def step(position, carry):
        now = position % 3
        after = (position + 1) % 3
        last = (position + 2) % 3
        spread_in = pltpu.make_async_copy(spreads_hbm.at[position], spread_buf, local_sem.at[4])
        snap_in = pltpu.make_async_copy(snaps_hbm.at[position], snap_buf, local_sem.at[5])
        spread_in.start()
        snap_in.start()
        for side in range(4):
            @pl.when(has[side])
            def _():
                copy_to(now, side).start()

        spread_in.wait()
        source_ref[...] = jnp.dot(plane_ref[...], spread_buf[...], preferred_element_type=jnp.float32)

        for zone, side in enumerate(zone_of):
            @pl.when(has[zone])
            def _():
                copy_to(now, side).wait_recv()
        snap_in.wait()

        def row(x, inner):
            center = ext_x[now, x + HALO]
            summed = 3.0 * stencil_weights[0] * center
            for offset in range(1, 5):
                along_x = ext_x[now, x + HALO + offset] + ext_x[now, x + HALO - offset]
                along_y = (
                    ext_y[now, x, pl.ds(2 * HALO + offset, width_y), :]
                    + ext_y[now, x, pl.ds(2 * HALO - offset, width_y), :]
                )
                above = jnp.where(lane < column - offset, pltpu.roll(center, column - offset, 1), 0.0)
                below = jnp.where(lane >= offset, pltpu.roll(center, offset, 1), 0.0)
                summed = summed + stencil_weights[offset] * (along_x + along_y + (above + below))
            rows = pl.ds(pl.multiple_of(x * width_y, width_y), width_y)
            source = (
                source_ref[rows, pl.ds(0, column)] + source_ref[rows, pl.ds(column, column)]
            ) + source_ref[rows, pl.ds(2 * column, column)]
            following = 2.0 * center - ext_x[last, x + HALO] + courant_ref[x] * (summed + source)
            ext_x[after, x + HALO] = following
            ext_y[after, x, mid_y, :] = following
            image_out_ref[x] = image_out_ref[x] + snap_buf[x].astype(jnp.float32) * following
            return inner

        lax.fori_loop(0, width_x, row, 0, unroll=2)

        for side in range(4):
            @pl.when(has[side])
            def _():
                copy_to(now, side).wait_send()
        return carry

    lax.fori_loop(0, steps, step, 0)

    ends = (
        pltpu.make_async_copy(ext_x.at[steps % 3, mid_x], field_ref, local_sem.at[0]),
        pltpu.make_async_copy(ext_x.at[(steps - 1) % 3, mid_x], before_ref, local_sem.at[1]),
    )
    for copy in ends:
        copy.start()
    for copy in ends:
        copy.wait()


def whole_window(now, before, courant, imaging, at_plane, snaps, spreads):
    grid_x, grid_y = lax.axis_size("gx"), lax.axis_size("gy")
    width_x, width_y, column = now.shape
    field = jax.ShapeDtypeStruct(now.shape, jnp.float32)
    vmem = pl.BlockSpec(memory_space=pltpu.VMEM)
    hbm = pl.BlockSpec(memory_space=pl.ANY)
    return pl.pallas_call(
        functools.partial(window_kernel, grid_x, grid_y),
        out_shape=(field, field, field),
        in_specs=[vmem] * 5 + [hbm, hbm],
        out_specs=(vmem, vmem, vmem),
        scratch_shapes=[
            pltpu.VMEM((3, width_x + 2 * HALO, width_y, column), jnp.float32),
            pltpu.VMEM((3, width_x, width_y + 4 * HALO, column), jnp.float32),
            pltpu.VMEM((width_x * width_y, 3 * column), jnp.float32),
            pltpu.VMEM(spreads.shape[1:], spreads.dtype),
            pltpu.VMEM(snaps.shape[1:], snaps.dtype),
            pltpu.SemaphoreType.DMA((4,)),
            pltpu.SemaphoreType.DMA((3, 4)),
            pltpu.SemaphoreType.DMA((6,)),
        ],
        compiler_params=pltpu.CompilerParams(
            collective_id=0, has_side_effects=True, vmem_limit_bytes=60 * 1024 * 1024
        ),
    )(now, before, courant, imaging, at_plane, snaps, spreads)


def split_high(value):
    scaled = value * 65537.0
    return scaled - (scaled - value)


def laplace(center, x_lo, x_hi, y_lo, y_hi):
    width_x, width_y, column = center.shape
    along_x_src = jnp.concatenate([x_lo, center, x_hi], axis=0)
    along_y_src = jnp.concatenate([y_lo, center, y_hi], axis=1)
    z_padded = jnp.pad(center, ((0, 0), (0, 0), (4, 4)))
    summed = 3.0 * stencil_weights[0] * center
    for offset in range(1, 5):
        along_x = (
            along_x_src[4 + offset : 4 + offset + width_x]
            + along_x_src[4 - offset : 4 - offset + width_x]
        )
        along_y = (
            along_y_src[:, 4 + offset : 4 + offset + width_y]
            + along_y_src[:, 4 - offset : 4 - offset + width_y]
        )
        along_z = (
            z_padded[:, :, 4 + offset : 4 + offset + column]
            + z_padded[:, :, 4 - offset : 4 - offset + column]
        )
        summed = summed + stencil_weights[offset] * (along_x + along_y + along_z)
    return summed


def per_device(
    observed,
    synthetic,
    match_filter,
    trace_shot,
    trace_owner,
    trace_cell,
    courant,
    adjoint_now,
    adjoint_prev,
    forward_field,
    image_start,
):
    trace_rows = observed.shape[1]
    grid_x = lax.axis_size("gx")
    grid_y = lax.axis_size("gy")
    devices = grid_x * grid_y
    capacity = max(2, 2 * trace_rows // devices)
    slot_count = devices * capacity
    shot_match = (trace_shot[:, None] == jnp.arange(SHOTS, dtype=jnp.int32)[None, :]).astype(
        jnp.float32
    )
    filters = jnp.dot(match_filter.T, shot_match.T, precision=lax.Precision.HIGHEST)
    residual = -observed
    for lag_index in range(TAPS):
        residual = (
            residual
            + filters[lag_index][None, :] * synthetic[STEPS - lag_index : 2 * STEPS - lag_index]
        )
    owners = trace_owner[:, 0]
    same_owner = owners[:, None] == owners[None, :]
    row_ids = jnp.arange(trace_rows, dtype=jnp.int32)
    earlier = row_ids[None, :] < row_ids[:, None]
    ranks = jnp.sum((same_owner & earlier).astype(jnp.int32), axis=1)
    slot_index = owners * capacity + ranks
    slot_table = (slot_index[:, None] == jnp.arange(slot_count, dtype=jnp.int32)[None, :]).astype(
        jnp.float32
    )
    payload = jnp.concatenate([residual, trace_cell.astype(jnp.float32)[None, :]], axis=0)
    parcel = jnp.dot(payload, slot_table, precision=lax.Precision.HIGHEST)
    received = lax.all_to_all(parcel, ("gx", "gy"), split_axis=1, concat_axis=1, tiled=True)
    got_values = received[:STEPS][::-1]
    got_cells = received[STEPS].astype(jnp.int32)
    plane = courant.shape[0] * courant.shape[1]
    column = courant.shape[2]
    got_plane = got_cells // column
    got_depth = got_cells % column
    at_plane = (got_plane[None, :] == jnp.arange(plane, dtype=jnp.int32)[:, None]).astype(jnp.bfloat16)
    at_depth = got_depth[:, None] == jnp.arange(column, dtype=jnp.int32)[None, :]
    top = split_high(got_values)
    rest = got_values - top
    second = split_high(rest)
    pieces = jnp.stack([top, second, rest - second], axis=2).astype(jnp.bfloat16)

    spreads = jnp.concatenate(
        [
            jnp.where(at_depth[None], pieces[:, :, j, None], jnp.zeros((), jnp.bfloat16))
            for j in range(3)
        ],
        axis=2,
    )
    current, before, imaging = whole_window(
        adjoint_now, adjoint_prev, courant, image_start, at_plane, forward_field, spreads
    )
    return (current, before, imaging)


def solution(mesh):
    return jax.shard_map(
        per_device,
        mesh=mesh,
        in_specs=(
            P(None, ("gx", "gy")),
            P(None, ("gx", "gy")),
            P(),
            P(("gx", "gy")),
            P(("gx", "gy"), None),
            P(("gx", "gy")),
            P("gx", "gy", None),
            P("gx", "gy", None),
            P("gx", "gy", None),
            P(None, "gx", "gy", None),
            P("gx", "gy", None),
        ),
        out_specs=(P("gx", "gy", None), P("gx", "gy", None), P("gx", "gy", None)),
        check_vma=False,
    )
```

```python
import functools

import jax
import jax.numpy as jnp
from jax import lax
from jax.experimental import pallas as pl
from jax.experimental.pallas import tpu as pltpu
from jax.sharding import PartitionSpec as P

MESH = pl.DeviceIdType.MESH

STEPS = 16
SHOTS = 16
TAPS = 17
HALO = 4


stencil_weights = (-205.0 / 72.0, 8.0 / 5.0, -1.0 / 5.0, 8.0 / 315.0, -1.0 / 560.0)


def faces(value, axis, dim):
    peers, length = lax.axis_size(axis), value.shape[dim]
    up = [(i, i + 1) for i in range(peers - 1)]
    down = [(j, i) for i, j in up]
    last = lax.slice_in_dim(value, length - HALO, length, axis=dim)
    first = lax.slice_in_dim(value, 0, HALO, axis=dim)
    return lax.ppermute(last, axis, up), lax.ppermute(first, axis, down)


def window_kernel(
    grid_x, grid_y, now_ref, prev_ref, courant_ref, image_ref, plane_ref, snaps_hbm, spreads_hbm,
    field_ref, before_ref, image_out_ref,
    ext_x, ext_y, source_ref, spread_buf, snap_buf, send_sem, recv_sem, local_sem,
):
    me_x = lax.axis_index("gx")
    me_y = lax.axis_index("gy")
    width_x, width_y, column = now_ref.shape
    steps = snaps_hbm.shape[0]
    has = (me_x > 0, me_x < grid_x - 1, me_y > 0, me_y < grid_y - 1)
    peers = ((me_x - 1, me_y), (me_x + 1, me_y), (me_x, me_y - 1), (me_x, me_y + 1))
    count = sum(flag.astype(jnp.int32) for flag in has)
    mid_x = pl.ds(HALO, width_x)
    mid_y = pl.ds(2 * HALO, width_y)

    starts = (
        pltpu.make_async_copy(now_ref, ext_x.at[0, mid_x], local_sem.at[0]),
        pltpu.make_async_copy(now_ref, ext_y.at[0, :, mid_y], local_sem.at[1]),
        pltpu.make_async_copy(prev_ref, ext_x.at[2, mid_x], local_sem.at[2]),
        pltpu.make_async_copy(image_ref, image_out_ref, local_sem.at[3]),
    )
    for copy in starts:
        copy.start()

    def zones(slot):
        return (
            ext_x.at[slot, pl.ds(0, HALO)],
            ext_x.at[slot, pl.ds(HALO + width_x, HALO)],
            ext_y.at[slot, :, pl.ds(HALO, HALO)],
            ext_y.at[slot, :, pl.ds(2 * HALO + width_y, HALO)],
        )

    for slot in range(3):
        for zone in range(4):
            @pl.when(jnp.logical_not(has[zone]))
            def _():
                target = zones(slot)[zone]
                target[...] = jnp.zeros(target.shape, jnp.float32)

    for copy in starts:
        copy.wait()

    barrier = pltpu.get_barrier_semaphore()
    for flag, peer in zip(has, peers):
        @pl.when(flag)
        def _():
            pl.semaphore_signal(barrier, inc=1, device_id=peer, device_id_type=MESH)
    pl.semaphore_wait(barrier, count)

    zone_of = (1, 0, 3, 2)
    lane = lax.broadcasted_iota(jnp.int32, (width_y, column), 1)

    def copy_to(slot, side):
        faces = (
            ext_x.at[slot, pl.ds(HALO, HALO)],
            ext_x.at[slot, pl.ds(width_x, HALO)],
            ext_y.at[slot, :, pl.ds(2 * HALO, HALO)],
            ext_y.at[slot, :, pl.ds(HALO + width_y, HALO)],
        )
        zone = zone_of[side]
        return pltpu.make_async_remote_copy(
            src_ref=faces[side],
            dst_ref=zones(slot)[zone],
            send_sem=send_sem.at[slot, side],
            recv_sem=recv_sem.at[slot, zone],
            device_id=peers[side],
            device_id_type=MESH,
        )

    def band(now, after, last, x, low, size):
        ys = pl.ds(low, size)
        lane = lax.broadcasted_iota(jnp.int32, (size, column), 1)
        center = ext_x[now, x + HALO, ys, :]
        summed = 3.0 * stencil_weights[0] * center
        for offset in range(1, 5):
            along_x = ext_x[now, x + HALO + offset, ys, :] + ext_x[now, x + HALO - offset, ys, :]
            along_y = (
                ext_y[now, x, pl.ds(2 * HALO + low + offset, size), :]
                + ext_y[now, x, pl.ds(2 * HALO + low - offset, size), :]
            )
            above = jnp.where(lane < column - offset, pltpu.roll(center, column - offset, 1), 0.0)
            below = jnp.where(lane >= offset, pltpu.roll(center, offset, 1), 0.0)
            summed = summed + stencil_weights[offset] * (along_x + along_y + (above + below))
        rows = pl.ds(pl.multiple_of(x * width_y + low, 8), size)
        source = (
            source_ref[rows, pl.ds(0, column)] + source_ref[rows, pl.ds(column, column)]
        ) + source_ref[rows, pl.ds(2 * column, column)]
        following = 2.0 * center - ext_x[last, x + HALO, ys, :] + courant_ref[x, ys, :] * (
            summed + source
        )
        ext_x[after, x + HALO, ys, :] = following
        ext_y[after, x, pl.ds(2 * HALO + low, size), :] = following
        snap = snap_buf[x].astype(jnp.float32)[low : low + size]
        image_out_ref[x, ys, :] = image_out_ref[x, ys, :] + snap * following

    for side in range(4):
        @pl.when(has[side])
        def _():
            copy_to(0, side).start()

    def step(position, carry):
        now = position % 3
        after = (position + 1) % 3
        last = (position + 2) % 3
        spread_in = pltpu.make_async_copy(spreads_hbm.at[position], spread_buf, local_sem.at[4])
        snap_in = pltpu.make_async_copy(snaps_hbm.at[position], snap_buf, local_sem.at[5])
        spread_in.start()
        snap_in.start()

        spread_in.wait()
        source_ref[...] = jnp.dot(plane_ref[...], spread_buf[...], preferred_element_type=jnp.float32)

        for zone, side in enumerate(zone_of):
            @pl.when(has[zone])
            def _():
                copy_to(now, side).wait_recv()
        snap_in.wait()

        def edges(x, inner):
            band(now, after, last, x, 0, 8)
            band(now, after, last, x, width_y - 8, 8)
            return inner

        lax.fori_loop(0, width_x, edges, 0)

        def face_rows(i, inner):
            x = jnp.where(i < HALO, i, i + width_x - 2 * HALO)
            band(now, after, last, x, 8, width_y - 16)
            return inner

        lax.fori_loop(0, 2 * HALO, face_rows, 0)

        @pl.when(position + 1 < steps)
        def _():
            for side in range(4):
                @pl.when(has[side])
                def _():
                    copy_to(after, side).start()

        def inside(x, inner):
            band(now, after, last, x, 8, width_y - 16)
            return inner

        lax.fori_loop(HALO, width_x - HALO, inside, 0)

        for side in range(4):
            @pl.when(has[side])
            def _():
                copy_to(now, side).wait_send()
        return carry

    lax.fori_loop(0, steps, step, 0)

    ends = (
        pltpu.make_async_copy(ext_x.at[steps % 3, mid_x], field_ref, local_sem.at[0]),
        pltpu.make_async_copy(ext_x.at[(steps - 1) % 3, mid_x], before_ref, local_sem.at[1]),
    )
    for copy in ends:
        copy.start()
    for copy in ends:
        copy.wait()


def whole_window(now, before, courant, imaging, at_plane, snaps, spreads):
    grid_x, grid_y = lax.axis_size("gx"), lax.axis_size("gy")
    width_x, width_y, column = now.shape
    field = jax.ShapeDtypeStruct(now.shape, jnp.float32)
    vmem = pl.BlockSpec(memory_space=pltpu.VMEM)
    hbm = pl.BlockSpec(memory_space=pl.ANY)
    return pl.pallas_call(
        functools.partial(window_kernel, grid_x, grid_y),
        out_shape=(field, field, field),
        in_specs=[vmem] * 5 + [hbm, hbm],
        out_specs=(vmem, vmem, vmem),
        scratch_shapes=[
            pltpu.VMEM((3, width_x + 2 * HALO, width_y, column), jnp.float32),
            pltpu.VMEM((3, width_x, width_y + 4 * HALO, column), jnp.float32),
            pltpu.VMEM((width_x * width_y, 3 * column), jnp.float32),
            pltpu.VMEM(spreads.shape[1:], spreads.dtype),
            pltpu.VMEM(snaps.shape[1:], snaps.dtype),
            pltpu.SemaphoreType.DMA((3, 4)),
            pltpu.SemaphoreType.DMA((3, 4)),
            pltpu.SemaphoreType.DMA((6,)),
        ],
        compiler_params=pltpu.CompilerParams(
            collective_id=0, has_side_effects=True, vmem_limit_bytes=60 * 1024 * 1024
        ),
    )(now, before, courant, imaging, at_plane, snaps, spreads)


def split_high(value):
    scaled = value * 65537.0
    return scaled - (scaled - value)


def laplace(center, x_lo, x_hi, y_lo, y_hi):
    width_x, width_y, column = center.shape
    along_x_src = jnp.concatenate([x_lo, center, x_hi], axis=0)
    along_y_src = jnp.concatenate([y_lo, center, y_hi], axis=1)
    z_padded = jnp.pad(center, ((0, 0), (0, 0), (4, 4)))
    summed = 3.0 * stencil_weights[0] * center
    for offset in range(1, 5):
        along_x = (
            along_x_src[4 + offset : 4 + offset + width_x]
            + along_x_src[4 - offset : 4 - offset + width_x]
        )
        along_y = (
            along_y_src[:, 4 + offset : 4 + offset + width_y]
            + along_y_src[:, 4 - offset : 4 - offset + width_y]
        )
        along_z = (
            z_padded[:, :, 4 + offset : 4 + offset + column]
            + z_padded[:, :, 4 - offset : 4 - offset + column]
        )
        summed = summed + stencil_weights[offset] * (along_x + along_y + along_z)
    return summed


def per_device(
    observed,
    synthetic,
    match_filter,
    trace_shot,
    trace_owner,
    trace_cell,
    courant,
    adjoint_now,
    adjoint_prev,
    forward_field,
    image_start,
):
    trace_rows = observed.shape[1]
    grid_x = lax.axis_size("gx")
    grid_y = lax.axis_size("gy")
    devices = grid_x * grid_y
    capacity = max(2, 2 * trace_rows // devices)
    slot_count = devices * capacity
    shot_match = (trace_shot[:, None] == jnp.arange(SHOTS, dtype=jnp.int32)[None, :]).astype(
        jnp.float32
    )
    filters = jnp.dot(match_filter.T, shot_match.T, precision=lax.Precision.HIGHEST)
    residual = -observed
    for lag_index in range(TAPS):
        residual = (
            residual
            + filters[lag_index][None, :] * synthetic[STEPS - lag_index : 2 * STEPS - lag_index]
        )
    owners = trace_owner[:, 0]
    same_owner = owners[:, None] == owners[None, :]
    row_ids = jnp.arange(trace_rows, dtype=jnp.int32)
    earlier = row_ids[None, :] < row_ids[:, None]
    ranks = jnp.sum((same_owner & earlier).astype(jnp.int32), axis=1)
    slot_index = owners * capacity + ranks
    slot_table = (slot_index[:, None] == jnp.arange(slot_count, dtype=jnp.int32)[None, :]).astype(
        jnp.float32
    )
    payload = jnp.concatenate([residual, trace_cell.astype(jnp.float32)[None, :]], axis=0)
    parcel = jnp.dot(payload, slot_table, precision=lax.Precision.HIGHEST)
    received = lax.all_to_all(parcel, ("gx", "gy"), split_axis=1, concat_axis=1, tiled=True)
    got_values = received[:STEPS][::-1]
    got_cells = received[STEPS].astype(jnp.int32)
    plane = courant.shape[0] * courant.shape[1]
    column = courant.shape[2]
    got_plane = got_cells // column
    got_depth = got_cells % column
    at_plane = (got_plane[None, :] == jnp.arange(plane, dtype=jnp.int32)[:, None]).astype(jnp.bfloat16)
    at_depth = got_depth[:, None] == jnp.arange(column, dtype=jnp.int32)[None, :]
    top = split_high(got_values)
    rest = got_values - top
    second = split_high(rest)
    pieces = jnp.stack([top, second, rest - second], axis=2).astype(jnp.bfloat16)

    spreads = jnp.concatenate(
        [
            jnp.where(at_depth[None], pieces[:, :, j, None], jnp.zeros((), jnp.bfloat16))
            for j in range(3)
        ],
        axis=2,
    )
    current, before, imaging = whole_window(
        adjoint_now, adjoint_prev, courant, image_start, at_plane, forward_field, spreads
    )
    return (current, before, imaging)


def solution(mesh):
    return jax.shard_map(
        per_device,
        mesh=mesh,
        in_specs=(
            P(None, ("gx", "gy")),
            P(None, ("gx", "gy")),
            P(),
            P(("gx", "gy")),
            P(("gx", "gy"), None),
            P(("gx", "gy")),
            P("gx", "gy", None),
            P("gx", "gy", None),
            P("gx", "gy", None),
            P(None, "gx", "gy", None),
            P("gx", "gy", None),
        ),
        out_specs=(P("gx", "gy", None), P("gx", "gy", None), P("gx", "gy", None)),
        check_vma=False,
    )
```

```python
import functools

import jax
import jax.numpy as jnp
from jax import lax
from jax.experimental import pallas as pl
from jax.experimental.pallas import tpu as pltpu
from jax.sharding import PartitionSpec as P

MESH = pl.DeviceIdType.MESH

STEPS = 16
SHOTS = 16
TAPS = 17
HALO = 4


stencil_weights = (-205.0 / 72.0, 8.0 / 5.0, -1.0 / 5.0, 8.0 / 315.0, -1.0 / 560.0)


def faces(value, axis, dim):
    peers, length = lax.axis_size(axis), value.shape[dim]
    up = [(i, i + 1) for i in range(peers - 1)]
    down = [(j, i) for i, j in up]
    last = lax.slice_in_dim(value, length - HALO, length, axis=dim)
    first = lax.slice_in_dim(value, 0, HALO, axis=dim)
    return lax.ppermute(last, axis, up), lax.ppermute(first, axis, down)


def window_kernel(
    grid_x, grid_y, now_ref, prev_ref, courant_ref, image_ref, plane_ref, pieces_ref, depth_ref,
    snaps_hbm, field_ref, before_ref, image_out_ref,
    ext_x, ext_y, source_ref, weighted, snap_buf, send_sem, recv_sem, local_sem,
):
    me_x = lax.axis_index("gx")
    me_y = lax.axis_index("gy")
    width_x, width_y, column = now_ref.shape
    steps = snaps_hbm.shape[0]
    has = (me_x > 0, me_x < grid_x - 1, me_y > 0, me_y < grid_y - 1)
    peers = ((me_x - 1, me_y), (me_x + 1, me_y), (me_x, me_y - 1), (me_x, me_y + 1))
    count = sum(flag.astype(jnp.int32) for flag in has)
    mid_x = pl.ds(HALO, width_x)
    mid_y = pl.ds(2 * HALO, width_y)

    starts = (
        pltpu.make_async_copy(now_ref, ext_x.at[0, mid_x], local_sem.at[0]),
        pltpu.make_async_copy(now_ref, ext_y.at[0, :, mid_y], local_sem.at[1]),
        pltpu.make_async_copy(prev_ref, ext_x.at[2, mid_x], local_sem.at[2]),
        pltpu.make_async_copy(image_ref, image_out_ref, local_sem.at[3]),
    )
    for copy in starts:
        copy.start()

    def zones(slot):
        return (
            ext_x.at[slot, pl.ds(0, HALO)],
            ext_x.at[slot, pl.ds(HALO + width_x, HALO)],
            ext_y.at[slot, :, pl.ds(HALO, HALO)],
            ext_y.at[slot, :, pl.ds(2 * HALO + width_y, HALO)],
        )

    for slot in range(3):
        for zone in range(4):
            @pl.when(jnp.logical_not(has[zone]))
            def _():
                target = zones(slot)[zone]
                target[...] = jnp.zeros(target.shape, jnp.float32)

    for copy in starts:
        copy.wait()

    barrier = pltpu.get_barrier_semaphore()
    for flag, peer in zip(has, peers):
        @pl.when(flag)
        def _():
            pl.semaphore_signal(barrier, inc=1, device_id=peer, device_id_type=MESH)
    pl.semaphore_wait(barrier, count)

    zone_of = (1, 0, 3, 2)
    lane = lax.broadcasted_iota(jnp.int32, (width_y, column), 1)

    def copy_to(slot, side):
        faces = (
            ext_x.at[slot, pl.ds(HALO, HALO)],
            ext_x.at[slot, pl.ds(width_x, HALO)],
            ext_y.at[slot, :, pl.ds(2 * HALO, HALO)],
            ext_y.at[slot, :, pl.ds(HALO + width_y, HALO)],
        )
        zone = zone_of[side]
        return pltpu.make_async_remote_copy(
            src_ref=faces[side],
            dst_ref=zones(slot)[zone],
            send_sem=send_sem.at[side],
            recv_sem=recv_sem.at[slot, zone],
            device_id=peers[side],
            device_id_type=MESH,
        )

    def step(position, carry):
        now = position % 3
        after = (position + 1) % 3
        last = (position + 2) % 3
        snap_in = pltpu.make_async_copy(snaps_hbm.at[position], snap_buf, local_sem.at[5])
        snap_in.start()
        for side in range(4):
            @pl.when(has[side])
            def _():
                copy_to(now, side).start()

        slots = plane_ref.shape[1]
        for piece in range(3):
            weighted[:, pl.ds(piece * slots, slots)] = (
                plane_ref[...] * pieces_ref[position, pl.ds(piece, 1), :]
            )
        source_ref[...] = jnp.dot(weighted[...], depth_ref[...], preferred_element_type=jnp.float32)

        for zone, side in enumerate(zone_of):
            @pl.when(has[zone])
            def _():
                copy_to(now, side).wait_recv()
        snap_in.wait()

        def row(x, inner):
            center = ext_x[now, x + HALO]
            summed = 3.0 * stencil_weights[0] * center
            for offset in range(1, 5):
                along_x = ext_x[now, x + HALO + offset] + ext_x[now, x + HALO - offset]
                along_y = (
                    ext_y[now, x, pl.ds(2 * HALO + offset, width_y), :]
                    + ext_y[now, x, pl.ds(2 * HALO - offset, width_y), :]
                )
                above = jnp.where(lane < column - offset, pltpu.roll(center, column - offset, 1), 0.0)
                below = jnp.where(lane >= offset, pltpu.roll(center, offset, 1), 0.0)
                summed = summed + stencil_weights[offset] * (along_x + along_y + (above + below))
            rows = pl.ds(pl.multiple_of(x * width_y, width_y), width_y)
            source = source_ref[rows, :]
            following = 2.0 * center - ext_x[last, x + HALO] + courant_ref[x] * (summed + source)
            ext_x[after, x + HALO] = following
            ext_y[after, x, mid_y, :] = following
            image_out_ref[x] = image_out_ref[x] + snap_buf[x].astype(jnp.float32) * following
            return inner

        lax.fori_loop(0, width_x, row, 0, unroll=2)

        for side in range(4):
            @pl.when(has[side])
            def _():
                copy_to(now, side).wait_send()
        return carry

    lax.fori_loop(0, steps, step, 0)

    ends = (
        pltpu.make_async_copy(ext_x.at[steps % 3, mid_x], field_ref, local_sem.at[0]),
        pltpu.make_async_copy(ext_x.at[(steps - 1) % 3, mid_x], before_ref, local_sem.at[1]),
    )
    for copy in ends:
        copy.start()
    for copy in ends:
        copy.wait()


def whole_window(now, before, courant, imaging, at_plane, pieces, at_depth, snaps):
    grid_x, grid_y = lax.axis_size("gx"), lax.axis_size("gy")
    width_x, width_y, column = now.shape
    field = jax.ShapeDtypeStruct(now.shape, jnp.float32)
    vmem = pl.BlockSpec(memory_space=pltpu.VMEM)
    hbm = pl.BlockSpec(memory_space=pl.ANY)
    return pl.pallas_call(
        functools.partial(window_kernel, grid_x, grid_y),
        out_shape=(field, field, field),
        in_specs=[vmem] * 7 + [hbm],
        out_specs=(vmem, vmem, vmem),
        scratch_shapes=[
            pltpu.VMEM((3, width_x + 2 * HALO, width_y, column), jnp.float32),
            pltpu.VMEM((3, width_x, width_y + 4 * HALO, column), jnp.float32),
            pltpu.VMEM((width_x * width_y, column), jnp.float32),
            pltpu.VMEM((width_x * width_y, 3 * at_plane.shape[1]), jnp.bfloat16),
            pltpu.VMEM(snaps.shape[1:], snaps.dtype),
            pltpu.SemaphoreType.DMA((4,)),
            pltpu.SemaphoreType.DMA((3, 4)),
            pltpu.SemaphoreType.DMA((6,)),
        ],
        compiler_params=pltpu.CompilerParams(
            collective_id=0, has_side_effects=True, vmem_limit_bytes=60 * 1024 * 1024
        ),
    )(now, before, courant, imaging, at_plane, pieces, at_depth, snaps)


def split_high(value):
    scaled = value * 65537.0
    return scaled - (scaled - value)


def laplace(center, x_lo, x_hi, y_lo, y_hi):
    width_x, width_y, column = center.shape
    along_x_src = jnp.concatenate([x_lo, center, x_hi], axis=0)
    along_y_src = jnp.concatenate([y_lo, center, y_hi], axis=1)
    z_padded = jnp.pad(center, ((0, 0), (0, 0), (4, 4)))
    summed = 3.0 * stencil_weights[0] * center
    for offset in range(1, 5):
        along_x = (
            along_x_src[4 + offset : 4 + offset + width_x]
            + along_x_src[4 - offset : 4 - offset + width_x]
        )
        along_y = (
            along_y_src[:, 4 + offset : 4 + offset + width_y]
            + along_y_src[:, 4 - offset : 4 - offset + width_y]
        )
        along_z = (
            z_padded[:, :, 4 + offset : 4 + offset + column]
            + z_padded[:, :, 4 - offset : 4 - offset + column]
        )
        summed = summed + stencil_weights[offset] * (along_x + along_y + along_z)
    return summed


def per_device(
    observed,
    synthetic,
    match_filter,
    trace_shot,
    trace_owner,
    trace_cell,
    courant,
    adjoint_now,
    adjoint_prev,
    forward_field,
    image_start,
):
    trace_rows = observed.shape[1]
    grid_x = lax.axis_size("gx")
    grid_y = lax.axis_size("gy")
    devices = grid_x * grid_y
    capacity = max(2, 2 * trace_rows // devices)
    slot_count = devices * capacity
    shot_match = (trace_shot[:, None] == jnp.arange(SHOTS, dtype=jnp.int32)[None, :]).astype(
        jnp.float32
    )
    filters = jnp.dot(match_filter.T, shot_match.T, precision=lax.Precision.HIGHEST)
    residual = -observed
    for lag_index in range(TAPS):
        residual = (
            residual
            + filters[lag_index][None, :] * synthetic[STEPS - lag_index : 2 * STEPS - lag_index]
        )
    owners = trace_owner[:, 0]
    same_owner = owners[:, None] == owners[None, :]
    row_ids = jnp.arange(trace_rows, dtype=jnp.int32)
    earlier = row_ids[None, :] < row_ids[:, None]
    ranks = jnp.sum((same_owner & earlier).astype(jnp.int32), axis=1)
    slot_index = owners * capacity + ranks
    slot_table = (slot_index[:, None] == jnp.arange(slot_count, dtype=jnp.int32)[None, :]).astype(
        jnp.float32
    )
    payload = jnp.concatenate([residual, trace_cell.astype(jnp.float32)[None, :]], axis=0)
    parcel = jnp.dot(payload, slot_table, precision=lax.Precision.HIGHEST)
    received = lax.all_to_all(parcel, ("gx", "gy"), split_axis=1, concat_axis=1, tiled=True)
    got_values = received[:STEPS][::-1]
    got_cells = received[STEPS].astype(jnp.int32)
    plane = courant.shape[0] * courant.shape[1]
    column = courant.shape[2]
    got_plane = got_cells // column
    got_depth = got_cells % column
    at_plane = (got_plane[None, :] == jnp.arange(plane, dtype=jnp.int32)[:, None]).astype(jnp.bfloat16)
    at_depth = got_depth[:, None] == jnp.arange(column, dtype=jnp.int32)[None, :]
    top = split_high(got_values)
    rest = got_values - top
    second = split_high(rest)
    pieces = jnp.stack([top, second, rest - second], axis=1).astype(jnp.bfloat16)

    at_depth = jnp.concatenate([at_depth.astype(jnp.bfloat16)] * 3, axis=0)
    current, before, imaging = whole_window(
        adjoint_now, adjoint_prev, courant, image_start, at_plane, pieces, at_depth, forward_field
    )
    return (current, before, imaging)


def solution(mesh):
    return jax.shard_map(
        per_device,
        mesh=mesh,
        in_specs=(
            P(None, ("gx", "gy")),
            P(None, ("gx", "gy")),
            P(),
            P(("gx", "gy")),
            P(("gx", "gy"), None),
            P(("gx", "gy")),
            P("gx", "gy", None),
            P("gx", "gy", None),
            P("gx", "gy", None),
            P(None, "gx", "gy", None),
            P("gx", "gy", None),
        ),
        out_specs=(P("gx", "gy", None), P("gx", "gy", None), P("gx", "gy", None)),
        check_vma=False,
    )
```

```python
import functools

import jax
import jax.numpy as jnp
from jax import lax
from jax.experimental import pallas as pl
from jax.experimental.pallas import tpu as pltpu
from jax.sharding import PartitionSpec as P

MESH = pl.DeviceIdType.MESH

STEPS = 16
SHOTS = 16
TAPS = 17
HALO = 4


stencil_weights = (-205.0 / 72.0, 8.0 / 5.0, -1.0 / 5.0, 8.0 / 315.0, -1.0 / 560.0)


def faces(value, axis, dim):
    peers, length = lax.axis_size(axis), value.shape[dim]
    up = [(i, i + 1) for i in range(peers - 1)]
    down = [(j, i) for i, j in up]
    last = lax.slice_in_dim(value, length - HALO, length, axis=dim)
    first = lax.slice_in_dim(value, 0, HALO, axis=dim)
    return lax.ppermute(last, axis, up), lax.ppermute(first, axis, down)


def window_kernel(
    grid_x, grid_y, now_ref, prev_ref, courant_ref, image_ref, plane_ref, pieces_ref, depth_ref,
    snaps_hbm, field_ref, before_ref, image_out_ref,
    ext_x, ext_y, source_ref, weighted, snap_buf, send_sem, recv_sem, local_sem,
):
    me_x = lax.axis_index("gx")
    me_y = lax.axis_index("gy")
    width_x, width_y, column = now_ref.shape
    steps = snaps_hbm.shape[0]
    has = (me_x > 0, me_x < grid_x - 1, me_y > 0, me_y < grid_y - 1)
    peers = ((me_x - 1, me_y), (me_x + 1, me_y), (me_x, me_y - 1), (me_x, me_y + 1))
    count = sum(flag.astype(jnp.int32) for flag in has)
    mid_x = pl.ds(HALO, width_x)
    mid_y = pl.ds(2 * HALO, width_y)

    starts = (
        pltpu.make_async_copy(now_ref, ext_x.at[0, mid_x], local_sem.at[0]),
        pltpu.make_async_copy(now_ref, ext_y.at[0, :, mid_y], local_sem.at[1]),
        pltpu.make_async_copy(prev_ref, ext_x.at[2, mid_x], local_sem.at[2]),
        pltpu.make_async_copy(image_ref, image_out_ref, local_sem.at[3]),
    )
    for copy in starts:
        copy.start()

    def zones(slot):
        return (
            ext_x.at[slot, pl.ds(0, HALO)],
            ext_x.at[slot, pl.ds(HALO + width_x, HALO)],
            ext_y.at[slot, :, pl.ds(HALO, HALO)],
            ext_y.at[slot, :, pl.ds(2 * HALO + width_y, HALO)],
        )

    for slot in range(3):
        for zone in range(4):
            @pl.when(jnp.logical_not(has[zone]))
            def _():
                target = zones(slot)[zone]
                target[...] = jnp.zeros(target.shape, jnp.float32)

    for copy in starts:
        copy.wait()

    barrier = pltpu.get_barrier_semaphore()
    for flag, peer in zip(has, peers):
        @pl.when(flag)
        def _():
            pl.semaphore_signal(barrier, inc=1, device_id=peer, device_id_type=MESH)
    pl.semaphore_wait(barrier, count)

    zone_of = (1, 0, 3, 2)
    lane = lax.broadcasted_iota(jnp.int32, (width_y, column), 1)

    def copy_to(slot, side):
        faces = (
            ext_x.at[slot, pl.ds(HALO, HALO)],
            ext_x.at[slot, pl.ds(width_x, HALO)],
            ext_y.at[slot, :, pl.ds(2 * HALO, HALO)],
            ext_y.at[slot, :, pl.ds(HALO + width_y, HALO)],
        )
        zone = zone_of[side]
        return pltpu.make_async_remote_copy(
            src_ref=faces[side],
            dst_ref=zones(slot)[zone],
            send_sem=send_sem.at[side],
            recv_sem=recv_sem.at[slot, zone],
            device_id=peers[side],
            device_id_type=MESH,
        )

    def step(position, carry):
        now = position % 3
        after = (position + 1) % 3
        last = (position + 2) % 3
        snap_in = pltpu.make_async_copy(snaps_hbm.at[position], snap_buf, local_sem.at[5])
        snap_in.start()
        for side in range(4):
            @pl.when(has[side])
            def _():
                copy_to(now, side).start()

        slots = plane_ref.shape[1]
        for piece in range(3):
            weighted[:, pl.ds(piece * slots, slots)] = (
                plane_ref[...] * pieces_ref[position, pl.ds(piece, 1), :]
            )
        source_ref[...] = jnp.dot(weighted[...], depth_ref[...], preferred_element_type=jnp.float32)

        for zone, side in enumerate(zone_of):
            @pl.when(has[zone])
            def _():
                copy_to(now, side).wait_recv()
        snap_in.wait()

        def row(x, inner):
            center = ext_x[now, x + HALO]
            summed = 3.0 * stencil_weights[0] * center
            for offset in range(1, 5):
                along_x = ext_x[now, x + HALO + offset] + ext_x[now, x + HALO - offset]
                along_y = (
                    ext_y[now, x, pl.ds(2 * HALO + offset, width_y), :]
                    + ext_y[now, x, pl.ds(2 * HALO - offset, width_y), :]
                )
                above = jnp.where(lane < column - offset, pltpu.roll(center, column - offset, 1), 0.0)
                below = jnp.where(lane >= offset, pltpu.roll(center, offset, 1), 0.0)
                summed = summed + stencil_weights[offset] * (along_x + along_y + (above + below))
            rows = pl.ds(pl.multiple_of(x * width_y, width_y), width_y)
            source = source_ref[rows, :]
            following = 2.0 * center - ext_x[last, x + HALO] + courant_ref[x] * (summed + source)
            ext_x[after, x + HALO] = following
            ext_y[after, x, mid_y, :] = following
            image_out_ref[x] = image_out_ref[x] + snap_buf[x].astype(jnp.float32) * following
            return inner

        lax.fori_loop(0, width_x, row, 0, unroll=2)

        for side in range(4):
            @pl.when(has[side])
            def _():
                copy_to(now, side).wait_send()
        return carry

    lax.fori_loop(0, steps, step, 0)

    ends = (
        pltpu.make_async_copy(ext_x.at[steps % 3, mid_x], field_ref, local_sem.at[0]),
        pltpu.make_async_copy(ext_x.at[(steps - 1) % 3, mid_x], before_ref, local_sem.at[1]),
    )
    for copy in ends:
        copy.start()
    for copy in ends:
        copy.wait()


def whole_window(now, before, courant, imaging, at_plane, pieces, at_depth, snaps):
    grid_x, grid_y = lax.axis_size("gx"), lax.axis_size("gy")
    width_x, width_y, column = now.shape
    field = jax.ShapeDtypeStruct(now.shape, jnp.float32)
    vmem = pl.BlockSpec(memory_space=pltpu.VMEM)
    hbm = pl.BlockSpec(memory_space=pl.ANY)
    return pl.pallas_call(
        functools.partial(window_kernel, grid_x, grid_y),
        out_shape=(field, field, field),
        in_specs=[vmem] * 7 + [hbm],
        out_specs=(vmem, vmem, vmem),
        scratch_shapes=[
            pltpu.VMEM((3, width_x + 2 * HALO, width_y, column), jnp.float32),
            pltpu.VMEM((3, width_x, width_y + 4 * HALO, column), jnp.float32),
            pltpu.VMEM((width_x * width_y, column), jnp.float32),
            pltpu.VMEM((width_x * width_y, 3 * at_plane.shape[1]), jnp.bfloat16),
            pltpu.VMEM(snaps.shape[1:], snaps.dtype),
            pltpu.SemaphoreType.DMA((4,)),
            pltpu.SemaphoreType.DMA((3, 4)),
            pltpu.SemaphoreType.DMA((6,)),
        ],
        compiler_params=pltpu.CompilerParams(
            collective_id=0, has_side_effects=True, vmem_limit_bytes=60 * 1024 * 1024
        ),
    )(now, before, courant, imaging, at_plane, pieces, at_depth, snaps)


def split_high(value):
    scaled = value * 65537.0
    return scaled - (scaled - value)


def laplace(center, x_lo, x_hi, y_lo, y_hi):
    width_x, width_y, column = center.shape
    along_x_src = jnp.concatenate([x_lo, center, x_hi], axis=0)
    along_y_src = jnp.concatenate([y_lo, center, y_hi], axis=1)
    z_padded = jnp.pad(center, ((0, 0), (0, 0), (4, 4)))
    summed = 3.0 * stencil_weights[0] * center
    for offset in range(1, 5):
        along_x = (
            along_x_src[4 + offset : 4 + offset + width_x]
            + along_x_src[4 - offset : 4 - offset + width_x]
        )
        along_y = (
            along_y_src[:, 4 + offset : 4 + offset + width_y]
            + along_y_src[:, 4 - offset : 4 - offset + width_y]
        )
        along_z = (
            z_padded[:, :, 4 + offset : 4 + offset + column]
            + z_padded[:, :, 4 - offset : 4 - offset + column]
        )
        summed = summed + stencil_weights[offset] * (along_x + along_y + along_z)
    return summed


def per_device(
    observed,
    synthetic,
    match_filter,
    trace_shot,
    trace_owner,
    trace_cell,
    courant,
    adjoint_now,
    adjoint_prev,
    forward_field,
    image_start,
):
    trace_rows = observed.shape[1]
    grid_x = lax.axis_size("gx")
    grid_y = lax.axis_size("gy")
    devices = grid_x * grid_y
    capacity = max(2, 2 * trace_rows // devices)
    slot_count = devices * capacity
    shot_match = (trace_shot[:, None] == jnp.arange(SHOTS, dtype=jnp.int32)[None, :]).astype(
        jnp.float32
    )
    filters = jnp.dot(match_filter.T, shot_match.T, precision=lax.Precision.HIGHEST)
    residual = -observed
    for lag_index in range(TAPS):
        residual = (
            residual
            + filters[lag_index][None, :] * synthetic[STEPS - lag_index : 2 * STEPS - lag_index]
        )
    owners = trace_owner[:, 0]
    same_owner = owners[:, None] == owners[None, :]
    row_ids = jnp.arange(trace_rows, dtype=jnp.int32)
    earlier = row_ids[None, :] < row_ids[:, None]
    ranks = jnp.sum((same_owner & earlier).astype(jnp.int32), axis=1)
    slot_index = owners * capacity + ranks
    slot_table = (slot_index[:, None] == jnp.arange(slot_count, dtype=jnp.int32)[None, :]).astype(
        jnp.float32
    )
    payload = jnp.concatenate([residual, trace_cell.astype(jnp.float32)[None, :]], axis=0)
    parcel = jnp.dot(payload, slot_table, precision=lax.Precision.HIGHEST)
    parcel = parcel.reshape(parcel.shape[0], grid_x, grid_y, capacity)
    parcel = lax.all_to_all(parcel, "gy", split_axis=2, concat_axis=2)
    parcel = lax.all_to_all(parcel, "gx", split_axis=1, concat_axis=1)
    received = parcel.reshape(parcel.shape[0], slot_count)
    got_values = received[:STEPS][::-1]
    got_cells = received[STEPS].astype(jnp.int32)
    plane = courant.shape[0] * courant.shape[1]
    column = courant.shape[2]
    got_plane = got_cells // column
    got_depth = got_cells % column
    at_plane = (got_plane[None, :] == jnp.arange(plane, dtype=jnp.int32)[:, None]).astype(jnp.bfloat16)
    at_depth = got_depth[:, None] == jnp.arange(column, dtype=jnp.int32)[None, :]
    top = split_high(got_values)
    rest = got_values - top
    second = split_high(rest)
    pieces = jnp.stack([top, second, rest - second], axis=1).astype(jnp.bfloat16)

    at_depth = jnp.concatenate([at_depth.astype(jnp.bfloat16)] * 3, axis=0)
    current, before, imaging = whole_window(
        adjoint_now, adjoint_prev, courant, image_start, at_plane, pieces, at_depth, forward_field
    )
    return (current, before, imaging)


def solution(mesh):
    return jax.shard_map(
        per_device,
        mesh=mesh,
        in_specs=(
            P(None, ("gx", "gy")),
            P(None, ("gx", "gy")),
            P(),
            P(("gx", "gy")),
            P(("gx", "gy"), None),
            P(("gx", "gy")),
            P("gx", "gy", None),
            P("gx", "gy", None),
            P("gx", "gy", None),
            P(None, "gx", "gy", None),
            P("gx", "gy", None),
        ),
        out_specs=(P("gx", "gy", None), P("gx", "gy", None), P("gx", "gy", None)),
        check_vma=False,
    )
```

```python
import functools

import jax
import jax.numpy as jnp
from jax import lax
from jax.experimental import pallas as pl
from jax.experimental.pallas import tpu as pltpu
from jax.sharding import PartitionSpec as P

MESH = pl.DeviceIdType.MESH

STEPS = 16
SHOTS = 16
TAPS = 17
HALO = 4


stencil_weights = (-205.0 / 72.0, 8.0 / 5.0, -1.0 / 5.0, 8.0 / 315.0, -1.0 / 560.0)


def faces(value, axis, dim):
    peers, length = lax.axis_size(axis), value.shape[dim]
    up = [(i, i + 1) for i in range(peers - 1)]
    down = [(j, i) for i, j in up]
    last = lax.slice_in_dim(value, length - HALO, length, axis=dim)
    first = lax.slice_in_dim(value, 0, HALO, axis=dim)
    return lax.ppermute(last, axis, up), lax.ppermute(first, axis, down)


def window_kernel(
    grid_x, grid_y, now_ref, prev_ref, courant_ref, image_ref, plane_of_ref, pieces_ref, depth_of_ref,
    snaps_hbm, field_ref, before_ref, image_out_ref,
    ext_x, ext_y, source_ref, weighted, snap_buf, plane_ref, depth_ref, send_sem, recv_sem, local_sem,
):
    me_x = lax.axis_index("gx")
    me_y = lax.axis_index("gy")
    width_x, width_y, column = now_ref.shape
    steps = snaps_hbm.shape[0]
    has = (me_x > 0, me_x < grid_x - 1, me_y > 0, me_y < grid_y - 1)
    peers = ((me_x - 1, me_y), (me_x + 1, me_y), (me_x, me_y - 1), (me_x, me_y + 1))
    count = sum(flag.astype(jnp.int32) for flag in has)
    mid_x = pl.ds(HALO, width_x)
    mid_y = pl.ds(2 * HALO, width_y)

    starts = (
        pltpu.make_async_copy(now_ref, ext_x.at[0, mid_x], local_sem.at[0]),
        pltpu.make_async_copy(now_ref, ext_y.at[0, :, mid_y], local_sem.at[1]),
        pltpu.make_async_copy(prev_ref, ext_x.at[2, mid_x], local_sem.at[2]),
        pltpu.make_async_copy(image_ref, image_out_ref, local_sem.at[3]),
    )
    for copy in starts:
        copy.start()

    def zones(slot):
        return (
            ext_x.at[slot, pl.ds(0, HALO)],
            ext_x.at[slot, pl.ds(HALO + width_x, HALO)],
            ext_y.at[slot, :, pl.ds(HALO, HALO)],
            ext_y.at[slot, :, pl.ds(2 * HALO + width_y, HALO)],
        )

    for slot in range(3):
        for zone in range(4):
            @pl.when(jnp.logical_not(has[zone]))
            def _():
                target = zones(slot)[zone]
                target[...] = jnp.zeros(target.shape, jnp.float32)

    plane_ref[...] = jnp.where(
        lax.broadcasted_iota(jnp.int32, plane_ref.shape, 0) == plane_of_ref[...], 1.0, 0.0
    ).astype(plane_ref.dtype)
    slots = plane_ref.shape[1]
    depth_hot = jnp.where(
        lax.broadcasted_iota(jnp.int32, (slots, column), 1) == depth_of_ref[...], 1.0, 0.0
    ).astype(depth_ref.dtype)
    for piece in range(3):
        depth_ref[pl.ds(piece * slots, slots), :] = depth_hot

    for copy in starts:
        copy.wait()

    barrier = pltpu.get_barrier_semaphore()
    for flag, peer in zip(has, peers):
        @pl.when(flag)
        def _():
            pl.semaphore_signal(barrier, inc=1, device_id=peer, device_id_type=MESH)
    pl.semaphore_wait(barrier, count)

    zone_of = (1, 0, 3, 2)
    lane = lax.broadcasted_iota(jnp.int32, (width_y, column), 1)

    def copy_to(slot, side):
        faces = (
            ext_x.at[slot, pl.ds(HALO, HALO)],
            ext_x.at[slot, pl.ds(width_x, HALO)],
            ext_y.at[slot, :, pl.ds(2 * HALO, HALO)],
            ext_y.at[slot, :, pl.ds(HALO + width_y, HALO)],
        )
        zone = zone_of[side]
        return pltpu.make_async_remote_copy(
            src_ref=faces[side],
            dst_ref=zones(slot)[zone],
            send_sem=send_sem.at[side],
            recv_sem=recv_sem.at[slot, zone],
            device_id=peers[side],
            device_id_type=MESH,
        )

    def step(position, carry):
        now = position % 3
        after = (position + 1) % 3
        last = (position + 2) % 3
        snap_in = pltpu.make_async_copy(snaps_hbm.at[position], snap_buf, local_sem.at[5])
        snap_in.start()
        for side in range(4):
            @pl.when(has[side])
            def _():
                copy_to(now, side).start()

        slots = plane_ref.shape[1]
        for piece in range(3):
            weighted[:, pl.ds(piece * slots, slots)] = (
                plane_ref[...] * pieces_ref[position, pl.ds(piece, 1), :]
            )
        source_ref[...] = jnp.dot(weighted[...], depth_ref[...], preferred_element_type=jnp.float32)

        for zone, side in enumerate(zone_of):
            @pl.when(has[zone])
            def _():
                copy_to(now, side).wait_recv()
        snap_in.wait()

        def row(x, inner):
            center = ext_x[now, x + HALO]
            summed = 3.0 * stencil_weights[0] * center
            for offset in range(1, 5):
                along_x = ext_x[now, x + HALO + offset] + ext_x[now, x + HALO - offset]
                along_y = (
                    ext_y[now, x, pl.ds(2 * HALO + offset, width_y), :]
                    + ext_y[now, x, pl.ds(2 * HALO - offset, width_y), :]
                )
                above = jnp.where(lane < column - offset, pltpu.roll(center, column - offset, 1), 0.0)
                below = jnp.where(lane >= offset, pltpu.roll(center, offset, 1), 0.0)
                summed = summed + stencil_weights[offset] * (along_x + along_y + (above + below))
            rows = pl.ds(pl.multiple_of(x * width_y, width_y), width_y)
            source = source_ref[rows, :]
            following = 2.0 * center - ext_x[last, x + HALO] + courant_ref[x] * (summed + source)
            ext_x[after, x + HALO] = following
            ext_y[after, x, mid_y, :] = following
            image_out_ref[x] = image_out_ref[x] + snap_buf[x].astype(jnp.float32) * following
            return inner

        lax.fori_loop(0, width_x, row, 0, unroll=2)

        for side in range(4):
            @pl.when(has[side])
            def _():
                copy_to(now, side).wait_send()
        return carry

    lax.fori_loop(0, steps, step, 0)

    ends = (
        pltpu.make_async_copy(ext_x.at[steps % 3, mid_x], field_ref, local_sem.at[0]),
        pltpu.make_async_copy(ext_x.at[(steps - 1) % 3, mid_x], before_ref, local_sem.at[1]),
    )
    for copy in ends:
        copy.start()
    for copy in ends:
        copy.wait()


def whole_window(now, before, courant, imaging, plane_of, pieces, depth_of, snaps):
    grid_x, grid_y = lax.axis_size("gx"), lax.axis_size("gy")
    width_x, width_y, column = now.shape
    field = jax.ShapeDtypeStruct(now.shape, jnp.float32)
    vmem = pl.BlockSpec(memory_space=pltpu.VMEM)
    hbm = pl.BlockSpec(memory_space=pl.ANY)
    return pl.pallas_call(
        functools.partial(window_kernel, grid_x, grid_y),
        out_shape=(field, field, field),
        in_specs=[vmem] * 7 + [hbm],
        out_specs=(vmem, vmem, vmem),
        scratch_shapes=[
            pltpu.VMEM((3, width_x + 2 * HALO, width_y, column), jnp.float32),
            pltpu.VMEM((3, width_x, width_y + 4 * HALO, column), jnp.float32),
            pltpu.VMEM((width_x * width_y, column), jnp.float32),
            pltpu.VMEM((width_x * width_y, 3 * plane_of.shape[1]), jnp.bfloat16),
            pltpu.VMEM(snaps.shape[1:], snaps.dtype),
            pltpu.VMEM((width_x * width_y, plane_of.shape[1]), jnp.bfloat16),
            pltpu.VMEM((3 * plane_of.shape[1], column), jnp.bfloat16),
            pltpu.SemaphoreType.DMA((4,)),
            pltpu.SemaphoreType.DMA((3, 4)),
            pltpu.SemaphoreType.DMA((6,)),
        ],
        compiler_params=pltpu.CompilerParams(
            collective_id=0, has_side_effects=True, vmem_limit_bytes=60 * 1024 * 1024
        ),
    )(now, before, courant, imaging, plane_of, pieces, depth_of, snaps)


def split_high(value):
    scaled = value * 65537.0
    return scaled - (scaled - value)


def laplace(center, x_lo, x_hi, y_lo, y_hi):
    width_x, width_y, column = center.shape
    along_x_src = jnp.concatenate([x_lo, center, x_hi], axis=0)
    along_y_src = jnp.concatenate([y_lo, center, y_hi], axis=1)
    z_padded = jnp.pad(center, ((0, 0), (0, 0), (4, 4)))
    summed = 3.0 * stencil_weights[0] * center
    for offset in range(1, 5):
        along_x = (
            along_x_src[4 + offset : 4 + offset + width_x]
            + along_x_src[4 - offset : 4 - offset + width_x]
        )
        along_y = (
            along_y_src[:, 4 + offset : 4 + offset + width_y]
            + along_y_src[:, 4 - offset : 4 - offset + width_y]
        )
        along_z = (
            z_padded[:, :, 4 + offset : 4 + offset + column]
            + z_padded[:, :, 4 - offset : 4 - offset + column]
        )
        summed = summed + stencil_weights[offset] * (along_x + along_y + along_z)
    return summed


def per_device(
    observed,
    synthetic,
    match_filter,
    trace_shot,
    trace_owner,
    trace_cell,
    courant,
    adjoint_now,
    adjoint_prev,
    forward_field,
    image_start,
):
    trace_rows = observed.shape[1]
    grid_x = lax.axis_size("gx")
    grid_y = lax.axis_size("gy")
    devices = grid_x * grid_y
    capacity = max(2, 2 * trace_rows // devices)
    slot_count = devices * capacity
    shot_match = (trace_shot[:, None] == jnp.arange(SHOTS, dtype=jnp.int32)[None, :]).astype(
        jnp.float32
    )
    filters = jnp.dot(match_filter.T, shot_match.T, precision=lax.Precision.HIGHEST)
    residual = -observed
    for lag_index in range(TAPS):
        residual = (
            residual
            + filters[lag_index][None, :] * synthetic[STEPS - lag_index : 2 * STEPS - lag_index]
        )
    owners = trace_owner[:, 0]
    same_owner = owners[:, None] == owners[None, :]
    row_ids = jnp.arange(trace_rows, dtype=jnp.int32)
    earlier = row_ids[None, :] < row_ids[:, None]
    ranks = jnp.sum((same_owner & earlier).astype(jnp.int32), axis=1)
    slot_index = owners * capacity + ranks
    slot_table = (slot_index[:, None] == jnp.arange(slot_count, dtype=jnp.int32)[None, :]).astype(
        jnp.float32
    )
    payload = jnp.concatenate([residual, trace_cell.astype(jnp.float32)[None, :]], axis=0)
    parcel = jnp.dot(payload, slot_table, precision=lax.Precision.HIGHEST)
    received = lax.all_to_all(parcel, ("gx", "gy"), split_axis=1, concat_axis=1, tiled=True)
    got_values = received[:STEPS][::-1]
    got_cells = received[STEPS].astype(jnp.int32)
    plane = courant.shape[0] * courant.shape[1]
    column = courant.shape[2]
    got_plane = got_cells // column
    got_depth = got_cells % column
    top = split_high(got_values)
    rest = got_values - top
    second = split_high(rest)
    pieces = jnp.stack([top, second, rest - second], axis=1).astype(jnp.bfloat16)

    current, before, imaging = whole_window(
        adjoint_now, adjoint_prev, courant, image_start, got_plane[None, :], pieces,
        got_depth[:, None], forward_field,
    )
    return (current, before, imaging)


def solution(mesh):
    return jax.shard_map(
        per_device,
        mesh=mesh,
        in_specs=(
            P(None, ("gx", "gy")),
            P(None, ("gx", "gy")),
            P(),
            P(("gx", "gy")),
            P(("gx", "gy"), None),
            P(("gx", "gy")),
            P("gx", "gy", None),
            P("gx", "gy", None),
            P("gx", "gy", None),
            P(None, "gx", "gy", None),
            P("gx", "gy", None),
        ),
        out_specs=(P("gx", "gy", None), P("gx", "gy", None), P("gx", "gy", None)),
        check_vma=False,
    )
```

```python
import functools

import jax
import jax.numpy as jnp
from jax import lax
from jax.experimental import pallas as pl
from jax.experimental.pallas import tpu as pltpu
from jax.sharding import PartitionSpec as P

MESH = pl.DeviceIdType.MESH

STEPS = 16
SHOTS = 16
TAPS = 17
HALO = 4


stencil_weights = (-205.0 / 72.0, 8.0 / 5.0, -1.0 / 5.0, 8.0 / 315.0, -1.0 / 560.0)


def faces(value, axis, dim):
    peers, length = lax.axis_size(axis), value.shape[dim]
    up = [(i, i + 1) for i in range(peers - 1)]
    down = [(j, i) for i, j in up]
    last = lax.slice_in_dim(value, length - HALO, length, axis=dim)
    first = lax.slice_in_dim(value, 0, HALO, axis=dim)
    return lax.ppermute(last, axis, up), lax.ppermute(first, axis, down)


def window_kernel(
    grid_x, grid_y, now_ref, prev_ref, courant_ref, image_ref, plane_ref, pieces_ref, depth_ref,
    snaps_hbm, field_ref, before_ref, image_out_ref,
    ext_x, ext_y, source_ref, weighted, snap_buf, send_sem, recv_sem, local_sem,
):
    me_x = lax.axis_index("gx")
    me_y = lax.axis_index("gy")
    width_x, width_y, column = now_ref.shape
    steps = snaps_hbm.shape[0]
    has = (me_x > 0, me_x < grid_x - 1, me_y > 0, me_y < grid_y - 1)
    peers = ((me_x - 1, me_y), (me_x + 1, me_y), (me_x, me_y - 1), (me_x, me_y + 1))
    count = sum(flag.astype(jnp.int32) for flag in has)
    mid_x = pl.ds(HALO, width_x)
    mid_y = pl.ds(2 * HALO, width_y)

    starts = (
        pltpu.make_async_copy(now_ref, ext_x.at[0, mid_x], local_sem.at[0]),
        pltpu.make_async_copy(now_ref, ext_y.at[0, :, mid_y], local_sem.at[1]),
        pltpu.make_async_copy(prev_ref, ext_x.at[2, mid_x], local_sem.at[2]),
        pltpu.make_async_copy(image_ref, image_out_ref, local_sem.at[3]),
    )
    for copy in starts:
        copy.start()

    def zones(slot):
        return (
            ext_x.at[slot, pl.ds(0, HALO)],
            ext_x.at[slot, pl.ds(HALO + width_x, HALO)],
            ext_y.at[slot, :, pl.ds(HALO, HALO)],
            ext_y.at[slot, :, pl.ds(2 * HALO + width_y, HALO)],
        )

    for slot in range(3):
        for zone in range(4):
            @pl.when(jnp.logical_not(has[zone]))
            def _():
                target = zones(slot)[zone]
                target[...] = jnp.zeros(target.shape, jnp.float32)

    for copy in starts:
        copy.wait()

    barrier = pltpu.get_barrier_semaphore()
    for flag, peer in zip(has, peers):
        @pl.when(flag)
        def _():
            pl.semaphore_signal(barrier, inc=1, device_id=peer, device_id_type=MESH)
    pl.semaphore_wait(barrier, count)

    zone_of = (1, 0, 3, 2)
    lane = lax.broadcasted_iota(jnp.int32, (width_y, column), 1)

    def copy_to(slot, side):
        faces = (
            ext_x.at[slot, pl.ds(HALO, HALO)],
            ext_x.at[slot, pl.ds(width_x, HALO)],
            ext_y.at[slot, :, pl.ds(2 * HALO, HALO)],
            ext_y.at[slot, :, pl.ds(HALO + width_y, HALO)],
        )
        zone = zone_of[side]
        return pltpu.make_async_remote_copy(
            src_ref=faces[side],
            dst_ref=zones(slot)[zone],
            send_sem=send_sem.at[slot, side],
            recv_sem=recv_sem.at[slot, zone],
            device_id=peers[side],
            device_id_type=MESH,
        )

    for side in (0, 1):
        @pl.when(has[side])
        def _():
            copy_to(0, side).start()

    def step(position, carry):
        now = position % 3
        after = (position + 1) % 3
        last = (position + 2) % 3
        snap_in = pltpu.make_async_copy(snaps_hbm.at[position], snap_buf, local_sem.at[5])
        snap_in.start()
        for side in (2, 3):
            @pl.when(has[side])
            def _():
                copy_to(now, side).start()

        slots = plane_ref.shape[1]
        for piece in range(3):
            weighted[:, pl.ds(piece * slots, slots)] = (
                plane_ref[...] * pieces_ref[position, pl.ds(piece, 1), :]
            )
        source_ref[...] = jnp.dot(weighted[...], depth_ref[...], preferred_element_type=jnp.float32)

        for zone, side in enumerate(zone_of):
            @pl.when(has[zone])
            def _():
                copy_to(now, side).wait_recv()
        snap_in.wait()

        def row(x, inner):
            center = ext_x[now, x + HALO]
            summed = 3.0 * stencil_weights[0] * center
            for offset in range(1, 5):
                along_x = ext_x[now, x + HALO + offset] + ext_x[now, x + HALO - offset]
                along_y = (
                    ext_y[now, x, pl.ds(2 * HALO + offset, width_y), :]
                    + ext_y[now, x, pl.ds(2 * HALO - offset, width_y), :]
                )
                above = jnp.where(lane < column - offset, pltpu.roll(center, column - offset, 1), 0.0)
                below = jnp.where(lane >= offset, pltpu.roll(center, offset, 1), 0.0)
                summed = summed + stencil_weights[offset] * (along_x + along_y + (above + below))
            rows = pl.ds(pl.multiple_of(x * width_y, width_y), width_y)
            source = source_ref[rows, :]
            following = 2.0 * center - ext_x[last, x + HALO] + courant_ref[x] * (summed + source)
            ext_x[after, x + HALO] = following
            ext_y[after, x, mid_y, :] = following
            image_out_ref[x] = image_out_ref[x] + snap_buf[x].astype(jnp.float32) * following
            return inner

        def face_row(i, inner):
            return row(jnp.where(i < HALO, i, i + width_x - 2 * HALO), inner)

        lax.fori_loop(0, 2 * HALO, face_row, 0)

        @pl.when(position + 1 < steps)
        def _():
            for side in (0, 1):
                @pl.when(has[side])
                def _():
                    copy_to(after, side).start()

        lax.fori_loop(HALO, width_x - HALO, row, 0, unroll=2)

        for side in range(4):
            @pl.when(has[side])
            def _():
                copy_to(now, side).wait_send()
        return carry

    lax.fori_loop(0, steps, step, 0)

    ends = (
        pltpu.make_async_copy(ext_x.at[steps % 3, mid_x], field_ref, local_sem.at[0]),
        pltpu.make_async_copy(ext_x.at[(steps - 1) % 3, mid_x], before_ref, local_sem.at[1]),
    )
    for copy in ends:
        copy.start()
    for copy in ends:
        copy.wait()


def whole_window(now, before, courant, imaging, at_plane, pieces, at_depth, snaps):
    grid_x, grid_y = lax.axis_size("gx"), lax.axis_size("gy")
    width_x, width_y, column = now.shape
    field = jax.ShapeDtypeStruct(now.shape, jnp.float32)
    vmem = pl.BlockSpec(memory_space=pltpu.VMEM)
    hbm = pl.BlockSpec(memory_space=pl.ANY)
    return pl.pallas_call(
        functools.partial(window_kernel, grid_x, grid_y),
        out_shape=(field, field, field),
        in_specs=[vmem] * 7 + [hbm],
        out_specs=(vmem, vmem, vmem),
        scratch_shapes=[
            pltpu.VMEM((3, width_x + 2 * HALO, width_y, column), jnp.float32),
            pltpu.VMEM((3, width_x, width_y + 4 * HALO, column), jnp.float32),
            pltpu.VMEM((width_x * width_y, column), jnp.float32),
            pltpu.VMEM((width_x * width_y, 3 * at_plane.shape[1]), jnp.bfloat16),
            pltpu.VMEM(snaps.shape[1:], snaps.dtype),
            pltpu.SemaphoreType.DMA((3, 4)),
            pltpu.SemaphoreType.DMA((3, 4)),
            pltpu.SemaphoreType.DMA((6,)),
        ],
        compiler_params=pltpu.CompilerParams(
            collective_id=0, has_side_effects=True, vmem_limit_bytes=60 * 1024 * 1024
        ),
    )(now, before, courant, imaging, at_plane, pieces, at_depth, snaps)


def split_high(value):
    scaled = value * 65537.0
    return scaled - (scaled - value)


def laplace(center, x_lo, x_hi, y_lo, y_hi):
    width_x, width_y, column = center.shape
    along_x_src = jnp.concatenate([x_lo, center, x_hi], axis=0)
    along_y_src = jnp.concatenate([y_lo, center, y_hi], axis=1)
    z_padded = jnp.pad(center, ((0, 0), (0, 0), (4, 4)))
    summed = 3.0 * stencil_weights[0] * center
    for offset in range(1, 5):
        along_x = (
            along_x_src[4 + offset : 4 + offset + width_x]
            + along_x_src[4 - offset : 4 - offset + width_x]
        )
        along_y = (
            along_y_src[:, 4 + offset : 4 + offset + width_y]
            + along_y_src[:, 4 - offset : 4 - offset + width_y]
        )
        along_z = (
            z_padded[:, :, 4 + offset : 4 + offset + column]
            + z_padded[:, :, 4 - offset : 4 - offset + column]
        )
        summed = summed + stencil_weights[offset] * (along_x + along_y + along_z)
    return summed


def per_device(
    observed,
    synthetic,
    match_filter,
    trace_shot,
    trace_owner,
    trace_cell,
    courant,
    adjoint_now,
    adjoint_prev,
    forward_field,
    image_start,
):
    trace_rows = observed.shape[1]
    grid_x = lax.axis_size("gx")
    grid_y = lax.axis_size("gy")
    devices = grid_x * grid_y
    capacity = max(2, 2 * trace_rows // devices)
    slot_count = devices * capacity
    shot_match = (trace_shot[:, None] == jnp.arange(SHOTS, dtype=jnp.int32)[None, :]).astype(
        jnp.float32
    )
    filters = jnp.dot(match_filter.T, shot_match.T, precision=lax.Precision.HIGHEST)
    residual = -observed
    for lag_index in range(TAPS):
        residual = (
            residual
            + filters[lag_index][None, :] * synthetic[STEPS - lag_index : 2 * STEPS - lag_index]
        )
    owners = trace_owner[:, 0]
    same_owner = owners[:, None] == owners[None, :]
    row_ids = jnp.arange(trace_rows, dtype=jnp.int32)
    earlier = row_ids[None, :] < row_ids[:, None]
    ranks = jnp.sum((same_owner & earlier).astype(jnp.int32), axis=1)
    slot_index = owners * capacity + ranks
    slot_table = (slot_index[:, None] == jnp.arange(slot_count, dtype=jnp.int32)[None, :]).astype(
        jnp.float32
    )
    payload = jnp.concatenate([residual, trace_cell.astype(jnp.float32)[None, :]], axis=0)
    parcel = jnp.dot(payload, slot_table, precision=lax.Precision.HIGHEST)
    received = lax.all_to_all(parcel, ("gx", "gy"), split_axis=1, concat_axis=1, tiled=True)
    got_values = received[:STEPS][::-1]
    got_cells = received[STEPS].astype(jnp.int32)
    plane = courant.shape[0] * courant.shape[1]
    column = courant.shape[2]
    got_plane = got_cells // column
    got_depth = got_cells % column
    at_plane = (got_plane[None, :] == jnp.arange(plane, dtype=jnp.int32)[:, None]).astype(jnp.bfloat16)
    at_depth = got_depth[:, None] == jnp.arange(column, dtype=jnp.int32)[None, :]
    top = split_high(got_values)
    rest = got_values - top
    second = split_high(rest)
    pieces = jnp.stack([top, second, rest - second], axis=1).astype(jnp.bfloat16)

    at_depth = jnp.concatenate([at_depth.astype(jnp.bfloat16)] * 3, axis=0)
    current, before, imaging = whole_window(
        adjoint_now, adjoint_prev, courant, image_start, at_plane, pieces, at_depth, forward_field
    )
    return (current, before, imaging)


def solution(mesh):
    return jax.shard_map(
        per_device,
        mesh=mesh,
        in_specs=(
            P(None, ("gx", "gy")),
            P(None, ("gx", "gy")),
            P(),
            P(("gx", "gy")),
            P(("gx", "gy"), None),
            P(("gx", "gy")),
            P("gx", "gy", None),
            P("gx", "gy", None),
            P("gx", "gy", None),
            P(None, "gx", "gy", None),
            P("gx", "gy", None),
        ),
        out_specs=(P("gx", "gy", None), P("gx", "gy", None), P("gx", "gy", None)),
        check_vma=False,
    )
```

```python
import functools

import jax
import jax.numpy as jnp
from jax import lax
from jax.experimental import pallas as pl
from jax.experimental.pallas import tpu as pltpu
from jax.sharding import PartitionSpec as P

MESH = pl.DeviceIdType.MESH

STEPS = 16
SHOTS = 16
TAPS = 17
HALO = 4


stencil_weights = (-205.0 / 72.0, 8.0 / 5.0, -1.0 / 5.0, 8.0 / 315.0, -1.0 / 560.0)


def faces(value, axis, dim):
    peers, length = lax.axis_size(axis), value.shape[dim]
    up = [(i, i + 1) for i in range(peers - 1)]
    down = [(j, i) for i, j in up]
    last = lax.slice_in_dim(value, length - HALO, length, axis=dim)
    first = lax.slice_in_dim(value, 0, HALO, axis=dim)
    return lax.ppermute(last, axis, up), lax.ppermute(first, axis, down)


def window_kernel(
    grid_x, grid_y, now_ref, prev_ref, courant_ref, image_ref, plane_ref, pieces_ref, depth_ref,
    snaps_hbm, field_ref, before_ref, image_out_ref,
    ext_x, ext_y, source_ref, weighted, snap_buf, send_sem, recv_sem, local_sem,
):
    me_x = lax.axis_index("gx")
    me_y = lax.axis_index("gy")
    width_x, width_y, column = now_ref.shape
    steps = snaps_hbm.shape[0]
    has = (me_x > 0, me_x < grid_x - 1, me_y > 0, me_y < grid_y - 1)
    peers = ((me_x - 1, me_y), (me_x + 1, me_y), (me_x, me_y - 1), (me_x, me_y + 1))
    count = sum(flag.astype(jnp.int32) for flag in has)
    mid_x = pl.ds(HALO, width_x)
    mid_y = pl.ds(2 * HALO, width_y)

    starts = (
        pltpu.make_async_copy(now_ref, ext_x.at[0, mid_x], local_sem.at[0]),
        pltpu.make_async_copy(now_ref, ext_y.at[0, :, mid_y], local_sem.at[1]),
        pltpu.make_async_copy(prev_ref, ext_x.at[2, mid_x], local_sem.at[2]),
        pltpu.make_async_copy(image_ref, image_out_ref, local_sem.at[3]),
    )
    for copy in starts:
        copy.start()

    def zones(slot):
        return (
            ext_x.at[slot, pl.ds(0, HALO)],
            ext_x.at[slot, pl.ds(HALO + width_x, HALO)],
            ext_y.at[slot, :, pl.ds(HALO, HALO)],
            ext_y.at[slot, :, pl.ds(2 * HALO + width_y, HALO)],
        )

    for slot in range(3):
        for zone in range(4):
            @pl.when(jnp.logical_not(has[zone]))
            def _():
                target = zones(slot)[zone]
                target[...] = jnp.zeros(target.shape, jnp.float32)

    for copy in starts:
        copy.wait()

    barrier = pltpu.get_barrier_semaphore()
    for flag, peer in zip(has, peers):
        @pl.when(flag)
        def _():
            pl.semaphore_signal(barrier, inc=1, device_id=peer, device_id_type=MESH)
    pl.semaphore_wait(barrier, count)

    zone_of = (1, 0, 3, 2)
    lane = lax.broadcasted_iota(jnp.int32, (width_y, column), 1)

    def copy_to(slot, side):
        faces = (
            ext_x.at[slot, pl.ds(HALO, HALO)],
            ext_x.at[slot, pl.ds(width_x, HALO)],
            ext_y.at[slot, :, pl.ds(2 * HALO, HALO)],
            ext_y.at[slot, :, pl.ds(HALO + width_y, HALO)],
        )
        zone = zone_of[side]
        return pltpu.make_async_remote_copy(
            src_ref=faces[side],
            dst_ref=zones(slot)[zone],
            send_sem=send_sem.at[slot, side],
            recv_sem=recv_sem.at[slot, zone],
            device_id=peers[side],
            device_id_type=MESH,
        )

    for side in range(4):
        @pl.when(has[side])
        def _():
            copy_to(0, side).start()

    def step(position, carry):
        now = position % 3
        after = (position + 1) % 3
        last = (position + 2) % 3
        snap_in = pltpu.make_async_copy(snaps_hbm.at[position], snap_buf, local_sem.at[5])
        snap_in.start()

        slots = plane_ref.shape[1]
        for piece in range(3):
            weighted[:, pl.ds(piece * slots, slots)] = (
                plane_ref[...] * pieces_ref[position, pl.ds(piece, 1), :]
            )
        source_ref[...] = jnp.dot(weighted[...], depth_ref[...], preferred_element_type=jnp.float32)

        for zone, side in enumerate(zone_of):
            @pl.when(has[zone])
            def _():
                copy_to(now, side).wait_recv()
        snap_in.wait()

        def row(x, inner):
            center = ext_x[now, x + HALO]
            summed = 3.0 * stencil_weights[0] * center
            for offset in range(1, 5):
                along_x = ext_x[now, x + HALO + offset] + ext_x[now, x + HALO - offset]
                along_y = (
                    ext_y[now, x, pl.ds(2 * HALO + offset, width_y), :]
                    + ext_y[now, x, pl.ds(2 * HALO - offset, width_y), :]
                )
                above = jnp.where(lane < column - offset, pltpu.roll(center, column - offset, 1), 0.0)
                below = jnp.where(lane >= offset, pltpu.roll(center, offset, 1), 0.0)
                summed = summed + stencil_weights[offset] * (along_x + along_y + (above + below))
            rows = pl.ds(pl.multiple_of(x * width_y, width_y), width_y)
            source = source_ref[rows, :]
            following = 2.0 * center - ext_x[last, x + HALO] + courant_ref[x] * (summed + source)
            ext_x[after, x + HALO] = following
            ext_y[after, x, mid_y, :] = following
            image_out_ref[x] = image_out_ref[x] + snap_buf[x].astype(jnp.float32) * following
            return inner

        def face_row(i, inner):
            return row(jnp.where(i < HALO, i, i + width_x - 2 * HALO), inner)

        lax.fori_loop(0, 2 * HALO, face_row, 0)

        @pl.when(position + 1 < steps)
        def _():
            for side in (0, 1):
                @pl.when(has[side])
                def _():
                    copy_to(after, side).start()

        lax.fori_loop(HALO, width_x - HALO, row, 0, unroll=2)

        @pl.when(position + 1 < steps)
        def _():
            for side in (2, 3):
                @pl.when(has[side])
                def _():
                    copy_to(after, side).start()

        for side in range(4):
            @pl.when(has[side])
            def _():
                copy_to(now, side).wait_send()
        return carry

    lax.fori_loop(0, steps, step, 0)

    ends = (
        pltpu.make_async_copy(ext_x.at[steps % 3, mid_x], field_ref, local_sem.at[0]),
        pltpu.make_async_copy(ext_x.at[(steps - 1) % 3, mid_x], before_ref, local_sem.at[1]),
    )
    for copy in ends:
        copy.start()
    for copy in ends:
        copy.wait()


def whole_window(now, before, courant, imaging, at_plane, pieces, at_depth, snaps):
    grid_x, grid_y = lax.axis_size("gx"), lax.axis_size("gy")
    width_x, width_y, column = now.shape
    field = jax.ShapeDtypeStruct(now.shape, jnp.float32)
    vmem = pl.BlockSpec(memory_space=pltpu.VMEM)
    hbm = pl.BlockSpec(memory_space=pl.ANY)
    return pl.pallas_call(
        functools.partial(window_kernel, grid_x, grid_y),
        out_shape=(field, field, field),
        in_specs=[vmem] * 7 + [hbm],
        out_specs=(vmem, vmem, vmem),
        scratch_shapes=[
            pltpu.VMEM((3, width_x + 2 * HALO, width_y, column), jnp.float32),
            pltpu.VMEM((3, width_x, width_y + 4 * HALO, column), jnp.float32),
            pltpu.VMEM((width_x * width_y, column), jnp.float32),
            pltpu.VMEM((width_x * width_y, 3 * at_plane.shape[1]), jnp.bfloat16),
            pltpu.VMEM(snaps.shape[1:], snaps.dtype),
            pltpu.SemaphoreType.DMA((3, 4)),
            pltpu.SemaphoreType.DMA((3, 4)),
            pltpu.SemaphoreType.DMA((6,)),
        ],
        compiler_params=pltpu.CompilerParams(
            collective_id=0, has_side_effects=True, vmem_limit_bytes=60 * 1024 * 1024
        ),
    )(now, before, courant, imaging, at_plane, pieces, at_depth, snaps)


def split_high(value):
    scaled = value * 65537.0
    return scaled - (scaled - value)


def laplace(center, x_lo, x_hi, y_lo, y_hi):
    width_x, width_y, column = center.shape
    along_x_src = jnp.concatenate([x_lo, center, x_hi], axis=0)
    along_y_src = jnp.concatenate([y_lo, center, y_hi], axis=1)
    z_padded = jnp.pad(center, ((0, 0), (0, 0), (4, 4)))
    summed = 3.0 * stencil_weights[0] * center
    for offset in range(1, 5):
        along_x = (
            along_x_src[4 + offset : 4 + offset + width_x]
            + along_x_src[4 - offset : 4 - offset + width_x]
        )
        along_y = (
            along_y_src[:, 4 + offset : 4 + offset + width_y]
            + along_y_src[:, 4 - offset : 4 - offset + width_y]
        )
        along_z = (
            z_padded[:, :, 4 + offset : 4 + offset + column]
            + z_padded[:, :, 4 - offset : 4 - offset + column]
        )
        summed = summed + stencil_weights[offset] * (along_x + along_y + along_z)
    return summed


def per_device(
    observed,
    synthetic,
    match_filter,
    trace_shot,
    trace_owner,
    trace_cell,
    courant,
    adjoint_now,
    adjoint_prev,
    forward_field,
    image_start,
):
    trace_rows = observed.shape[1]
    grid_x = lax.axis_size("gx")
    grid_y = lax.axis_size("gy")
    devices = grid_x * grid_y
    capacity = max(2, 2 * trace_rows // devices)
    slot_count = devices * capacity
    shot_match = (trace_shot[:, None] == jnp.arange(SHOTS, dtype=jnp.int32)[None, :]).astype(
        jnp.float32
    )
    filters = jnp.dot(match_filter.T, shot_match.T, precision=lax.Precision.HIGHEST)
    residual = -observed
    for lag_index in range(TAPS):
        residual = (
            residual
            + filters[lag_index][None, :] * synthetic[STEPS - lag_index : 2 * STEPS - lag_index]
        )
    owners = trace_owner[:, 0]
    same_owner = owners[:, None] == owners[None, :]
    row_ids = jnp.arange(trace_rows, dtype=jnp.int32)
    earlier = row_ids[None, :] < row_ids[:, None]
    ranks = jnp.sum((same_owner & earlier).astype(jnp.int32), axis=1)
    slot_index = owners * capacity + ranks
    slot_table = (slot_index[:, None] == jnp.arange(slot_count, dtype=jnp.int32)[None, :]).astype(
        jnp.float32
    )
    payload = jnp.concatenate([residual, trace_cell.astype(jnp.float32)[None, :]], axis=0)
    parcel = jnp.dot(payload, slot_table, precision=lax.Precision.HIGHEST)
    received = lax.all_to_all(parcel, ("gx", "gy"), split_axis=1, concat_axis=1, tiled=True)
    got_values = received[:STEPS][::-1]
    got_cells = received[STEPS].astype(jnp.int32)
    plane = courant.shape[0] * courant.shape[1]
    column = courant.shape[2]
    got_plane = got_cells // column
    got_depth = got_cells % column
    at_plane = (got_plane[None, :] == jnp.arange(plane, dtype=jnp.int32)[:, None]).astype(jnp.bfloat16)
    at_depth = got_depth[:, None] == jnp.arange(column, dtype=jnp.int32)[None, :]
    top = split_high(got_values)
    rest = got_values - top
    second = split_high(rest)
    pieces = jnp.stack([top, second, rest - second], axis=1).astype(jnp.bfloat16)

    at_depth = jnp.concatenate([at_depth.astype(jnp.bfloat16)] * 3, axis=0)
    current, before, imaging = whole_window(
        adjoint_now, adjoint_prev, courant, image_start, at_plane, pieces, at_depth, forward_field
    )
    return (current, before, imaging)


def solution(mesh):
    return jax.shard_map(
        per_device,
        mesh=mesh,
        in_specs=(
            P(None, ("gx", "gy")),
            P(None, ("gx", "gy")),
            P(),
            P(("gx", "gy")),
            P(("gx", "gy"), None),
            P(("gx", "gy")),
            P("gx", "gy", None),
            P("gx", "gy", None),
            P("gx", "gy", None),
            P(None, "gx", "gy", None),
            P("gx", "gy", None),
        ),
        out_specs=(P("gx", "gy", None), P("gx", "gy", None), P("gx", "gy", None)),
        check_vma=False,
    )
```
